128 devices in a mesh: dp: 8 (over x_lo, z), param: 16 (over x_hi, y, core).
Axes of the slice: x: 4 (x_hi: 2, x_lo: 2; x = x_hi * 2 + x_lo), y: 4, z: 4, core: 2. Of those that a mesh axis runs over, the one named last changes fastest.
Arguments:
- train_grads: bfloat16 [512, 262144], P('dp', 'param'), may hold values from -6 to 6
- target_grads: bfloat16 [256, 262144], P('dp', 'param'), may hold values from -6 to 6
- projection: bfloat16 [1024, 262144], P('dp', 'param'), may hold values from -0.01171875 to 0.01171875
- first_moment: float32 [16, 8, 2048], P('param', 'dp'), may hold values from -0.3 to 0.3
- second_moment: float32 [16, 8, 2048], P('param', 'dp'), may hold values from 0.001 to 0.1
- owner_map: int32 [16, 8], P('param'), may hold values from 0 to 7, as said below
Outputs:
- similarity: float32 [512, 256], P(('dp', 'param'))
The draws below stay inside these ranges and needn't reach their ends.
Inputs may be any that keep to these rules, and one draw needn't show every extreme that they name: `owner_map`: each row is a permutation of 0 to 7.
All inputs are finite; a program needn't handle non-finite values.
Results may differ from the reference program's by a relative error of at most 0.0029.
Values may be sent and summed in bfloat16 or wider, within the bound.
A program may use at most 128 MiB of HBM per device.

```python
import math
import jax
import jax.numpy as jnp
from jax import lax

K = 1024
TR_DEV = 64
P_SIZE = 262144
BLK = 2048
TRAIN = 512
TARGETS = 256
N_DP = 8
N_PARAM = 16


def draw_owner_map(key, part):
    row_keys = jax.random.split(jax.random.fold_in(key, 7), N_PARAM)
    return jax.vmap(lambda row_key: jax.random.permutation(row_key, N_DP))(row_keys).astype(jnp.int32)


def block_levels(key, shape, cuts, low, top_value):
    factor_of, own = 1.0, jax.random.fold_in(key, 6)
    for position, shards_of in cuts:
        heights = jnp.exp(jax.random.uniform(jax.random.fold_in(own, position), (shards_of,), jnp.float32, low / len(cuts), top_value / len(cuts)))
        factor_of = factor_of * jnp.repeat(heights, shape[position] // shards_of).reshape([-1 if axis == position else 1 for axis in range(len(shape))])
    return factor_of


def centred(key, extent, deviation, limit, cuts=(), held_as=jnp.bfloat16):
    result = jax.random.normal(key, extent, jnp.float32) * deviation
    if len(cuts) > 0:
        result = block_levels(key, extent, cuts, -0.22, 0.18) * result
    return jnp.clip(result, min=-limit, max=limit).astype(held_as)


def setup_inputs(seed: int = 0) -> dict:
    seeds = jax.random.split(jax.random.key(seed), 7)
    return {
        "train_grads": centred(seeds[0], (TRAIN, P_SIZE), 1.0, 6.0, ((0, 8), (1, 16))),
        "target_grads": centred(seeds[1], (TARGETS, P_SIZE), 1.0, 6.0, ((0, 8), (1, 16))),
        "projection": centred(seeds[2], (K, P_SIZE), P_SIZE ** -0.5, 0.01171875, ((0, 8), (1, 16))),
        "first_moment": centred(seeds[3], (N_PARAM, N_DP, BLK), 0.05, 0.3, ((0, 16), (1, 8)), jnp.float32),
        "second_moment": jnp.clip(jnp.exp(math.log(0.1) - 4.6051702 * jax.random.uniform(seeds[4], (N_PARAM, N_DP, BLK), jnp.float32) ** block_levels(seeds[4], (N_PARAM, N_DP, BLK), ((0, 16), (1, 8)), -0.2, 0.2)), 0.001, 0.1),
        "owner_map": draw_owner_map(jax.random.fold_in(seeds[6], 71), 0),
    }


def precondition(grad_rows, first_full, second_full):
    grad_f32 = grad_rows.astype(jnp.float32)
    upper = 0.9 * first_full + 0.1 * grad_f32
    lower = jnp.sqrt(0.999 * second_full + 0.001 * grad_f32 * grad_f32) + 1e-08
    return (upper / lower).astype(jnp.bfloat16)

def project(grad_rows, projection):
    return lax.dot_general(grad_rows, projection, (((1,), (1,)), ((), ())), preferred_element_type=jnp.float32)

def normalize(features):
    return features * lax.rsqrt(lax.optimization_barrier(jnp.mean(features * features, axis=1, keepdims=True)) + 1e-06)

def reference(train_grads, target_grads, projection, first_moment, second_moment, owner_map):
    group_ids = jnp.arange(N_PARAM).astype(jnp.int32)[:, None]
    owners = owner_map.astype(jnp.int32)
    first_full = first_moment[group_ids, owners].reshape(-1)
    second_full = second_moment[group_ids, owners].reshape(-1)

    def one_block(block_rows):
        return project(precondition(block_rows, first_full, second_full), projection)
    train_features = lax.map(one_block, train_grads.reshape(N_DP, TR_DEV, P_SIZE)).reshape(TRAIN, K)
    target_features = project(target_grads, projection)
    train_unit = normalize(train_features)
    target_unit = normalize(target_features)
    similarity = jnp.dot(train_unit, target_unit.T, precision=lax.Precision.HIGHEST, preferred_element_type=jnp.float32)
    return similarity / math.sqrt(K)
```

```python
import functools
import math

import jax
import jax.numpy as jnp
from jax import lax
from jax.experimental import pallas as pl
from jax.experimental.pallas import tpu as pltpu
from jax.sharding import PartitionSpec as P

MESH = pl.DeviceIdType.MESH
F32, BF16 = jnp.float32, jnp.bfloat16
COLS = 2048
FEATS = 1024
GROUPS = 6
TGROUPS = 2


def one_hot(rows, source_of):
    r = lax.broadcasted_iota(jnp.int32, (rows, rows), 0)
    s = lax.broadcasted_iota(jnp.int32, (rows, rows), 1)
    return jnp.where(source_of(r) == s, 1.0, 0.0).astype(BF16)


def bits(r, low, width):
    return (r >> low) & ((1 << width) - 1)


def kernel(
    train, target, proj, first, second, owners,
    out,
    raw_rows, raw_targets, sorted_rows, sorted_targets,
    all_proj, all_rows, all_first, all_second, mixed, lhs,
    partial, from_core, by_y, from_y, by_xz, from_xz, unit, unit_cat, own_rows,
    load_sem, mom_sem, proj_sem, row_sem, core_sem, y_sem, xz_sem, unit_sem,
):
    dp = lax.axis_index("dp")
    param = lax.axis_index("param")
    x_hi, y, core = param // 8, (param // 2) % 4, param % 2
    place = x_hi * 8 + dp

    def dp_peer(o):
        return (dp + o) % 8, {"dp": (dp + o) % 8, "param": param}

    core_peer = {"dp": dp, "param": x_hi * 8 + y * 2 + (1 - core)}

    def y_peer(o):
        other = (y + o) % 4
        return other, {"dp": dp, "param": x_hi * 8 + other * 2 + core}

    def xz_peer(o):
        far, near = (x_hi + o // 8) % 2, (dp + o % 8) % 8
        return far * 8 + near, {"dp": near, "param": far * 8 + y * 2 + core}

    def send(src, dst, sems, at, device):
        pltpu.make_async_remote_copy(
            src_ref=src, dst_ref=dst, send_sem=sems.at[0, at], recv_sem=sems.at[1, at],
            device_id=device, device_id_type=MESH,
        ).start()

    def keep(src, dst, sem):
        pltpu.make_async_copy(src, dst, sem).start()

    def wait(ref, sem):
        pltpu.make_async_copy(ref, ref, sem).wait()

    keep(target, raw_targets, load_sem.at[0])
    keep(train, raw_rows, load_sem.at[1])
    barrier = pltpu.get_barrier_semaphore()
    peers = [xz_peer(o)[1] for o in range(1, 16)] + [core_peer] + [y_peer(o)[1] for o in range(1, 4)]
    for device in peers:
        pl.semaphore_signal(barrier, inc=1, device_id=device, device_id_type=MESH)
    pl.semaphore_wait(barrier, len(peers))

    keep(first.at[0], all_first.at[dp], mom_sem.at[1, 0])
    keep(second.at[0], all_second.at[dp], mom_sem.at[1, 1])
    order = (2, 6, 5, 7, 1, 3, 4)
    for o in order:
        other, device = dp_peer(o)
        send(first.at[0], all_first.at[dp], mom_sem, 0, device)
        send(second.at[0], all_second.at[dp], mom_sem, 1, device)
    for o in order:
        other, device = dp_peer(o)
        send(proj.at[:, pl.ds(other * COLS, COLS)], all_proj.at[dp], proj_sem, 0, device)
    keep(proj.at[:, pl.ds(dp * COLS, COLS)], all_proj.at[dp], proj_sem.at[1, 0])

    def sort(raw, done, groups):
        rows = groups * 16
        pick = one_hot(rows, lambda r: (r & 15) * groups + (r >> 4))

        @pl.loop(0, 16)
        def _(t):
            cols = pl.ds(pl.multiple_of(t * 1024, 1024), 1024)
            done[:, cols] = jnp.dot(pick, raw[:, cols], preferred_element_type=F32).astype(BF16)

    def send_rows(k):
        done, at = (sorted_targets, k) if k < TGROUPS else (sorted_rows, k - TGROUPS)
        rows = pl.ds(at * 16, 16)
        for o in order:
            other, device = dp_peer(o)
            send(done.at[rows, pl.ds(other * COLS, COLS)], all_rows.at[k, dp], row_sem, k, device)
        keep(done.at[rows, pl.ds(dp * COLS, COLS)], all_rows.at[k, dp], row_sem.at[1, k])

    wait(raw_targets, load_sem.at[0])
    sort(raw_targets, sorted_targets, 2)
    wait(raw_rows, load_sem.at[1])
    sort(raw_rows, sorted_rows, 4)
    for k in range(GROUPS):
        send_rows(k)

    wait(all_first, mom_sem.at[1, 0])
    wait(all_second, mom_sem.at[1, 1])
    owner = owners[0, dp]
    first_row = 0.9 * all_first[owner]
    second_row = 0.999 * all_second[owner]

    regroup = one_hot(
        128, lambda r: bits(r, 0, 3) * 16 + bits(r, 3, 1) * 8 + bits(r, 4, 2) * 2 + bits(r, 6, 1)
    )

    def multiply(k):
        wait(all_rows.at[k], row_sem.at[1, k])
        if k >= TGROUPS:

            @pl.loop(0, 8)
            def _(s):
                for t in range(4):
                    cols = slice(t * 512, (t + 1) * 512)
                    g = all_rows[k, s, :, cols].astype(F32)
                    upper = first_row[:, cols] + 0.1 * g
                    lower = jnp.sqrt(second_row[:, cols] + 0.001 * g * g) + 1e-08
                    mixed[s, :, cols] = (upper / lower).astype(BF16)

        @pl.loop(0, 4)
        def _(t):
            cols = pl.ds(pl.multiple_of(t * 512, 512), 512)
            rows = mixed[:, :, cols] if k >= TGROUPS else all_rows[k, :, :, cols]
            lhs[:, cols] = jnp.dot(
                regroup, rows.reshape(128, 512), preferred_element_type=F32
            ).astype(BF16)

        @pl.loop(0, 4)
        def _(t):
            some = all_proj[pl.ds(t * 2, 2)].reshape(256, COLS)
            partial[k, :, pl.ds(pl.multiple_of(t * 256, 256), 256)] = lax.dot_general(
                lhs[...], some, (((1,), (1,)), ((), ())), preferred_element_type=F32
            )

        send(partial.at[k, pl.ds((1 - core) * 64, 64)], from_core.at[k], core_sem, k, core_peer)

    def add_core(k):
        wait(from_core.at[k], core_sem.at[1, k])

        @pl.loop(0, 4)
        def _(t):
            rows = pl.ds(t * 16, 16)
            by_y[k, rows] = partial[k, pl.ds(core * 64 + t * 16, 16)] + from_core[k, rows]

        for o in (2, 1, 3):
            other, device = y_peer(o)
            send(by_y.at[k, pl.ds(other * 16, 16)], from_y.at[k, o - 1], y_sem, k, device)

    def add_y(k):
        wait(from_y.at[k], y_sem.at[1, k])
        total = by_y[k, pl.ds(y * 16, 16)] + from_y[k, 0] + from_y[k, 1] + from_y[k, 2]
        for s in range(8):
            by_xz[k, pl.ds(s, 16, stride=8), :] = total[:, s * 128 : (s + 1) * 128]
        for o in range(1, 16):
            other, device = xz_peer(o)
            send(by_xz.at[k, pl.ds(other * 8, 8)], from_xz.at[k, pl.ds(o * 8 - 8, 8)], xz_sem, k, device)

    def unit_row(k):
        wait(from_xz.at[k], xz_sem.at[1, k])
        f = by_xz[k, pl.ds(place * 8, 8)]
        for o in range(15):
            f = f + from_xz[k, o * 8 : o * 8 + 8]
        mean = jnp.sum(f * f, keepdims=True) / FEATS
        return f * lax.rsqrt(mean + 1e-06)

    spot = (core * 4 + y) * 16 + place

    def target_row(k):
        unit[pl.ds(spot * 16 + k * 8, 8)] = unit_row(k)

    def train_row(k):
        own_rows[(k - TGROUPS) * 8 : (k - TGROUPS + 1) * 8] = unit_row(k)

    def gather_xz():
        mine = unit.at[pl.ds(spot * 16, 16)]
        for o in range(1, 16):
            send(mine, mine, unit_sem, 0, xz_peer(o)[1])

    def gather_y():
        wait(unit.at[pl.ds(0, 240)], unit_sem.at[1, 0])
        mine = unit.at[pl.ds((core * 4 + y) * 256, 256)]
        for o in (2, 1, 3):
            send(mine, mine, unit_sem, 1, y_peer(o)[1])

    def gather_core():
        wait(unit.at[pl.ds(0, 768)], unit_sem.at[1, 1])
        mine = unit.at[pl.ds(core * 1024, 1024)]
        send(mine, mine, unit_sem, 2, core_peer)

    def arrange():
        wait(unit.at[pl.ds(0, 1024)], unit_sem.at[1, 2])
        natural = one_hot(
            256,
            lambda r: bits(r, 1, 1) * 128 + bits(r, 2, 2) * 32 + bits(r, 4, 1) * 16
            + bits(r, 5, 3) * 2 + bits(r, 0, 1),
        )
        for s in range(8):
            piece = unit[pl.ds(s, 256, stride=8), :]
            high = piece.astype(BF16)
            low = (piece - high.astype(F32)).astype(BF16)
            cols = slice(s * 128, (s + 1) * 128)
            unit_cat[0:256, cols] = jnp.dot(natural, high, preferred_element_type=F32).astype(BF16)
            unit_cat[256:512, cols] = jnp.dot(natural, low, preferred_element_type=F32).astype(BF16)

    wait(all_proj, proj_sem.at[1, 0])
    own_rows[...] = jnp.zeros_like(own_rows)
    multiply(0)
    multiply(1)
    add_core(0)
    add_core(1)
    multiply(2)
    add_y(0)
    add_y(1)
    add_core(2)
    multiply(3)
    target_row(0)
    target_row(1)
    gather_xz()
    add_y(2)
    add_core(3)
    multiply(4)
    gather_y()
    train_row(2)
    add_y(3)
    add_core(4)
    multiply(5)
    gather_core()
    train_row(3)
    add_y(4)
    add_core(5)
    arrange()
    train_row(4)
    add_y(5)
    train_row(5)

    rows = jnp.concatenate([own_rows[pl.ds(s, 8, stride=8), :] for s in range(8)], axis=1)
    high = rows.astype(BF16)
    low = (rows - high.astype(F32)).astype(BF16)
    product = lax.dot_general(
        jnp.concatenate([high, low], axis=0), unit_cat[...], (((1,), (1,)), ((), ())),
        preferred_element_type=F32,
    )
    scaled = product[0:8, 0:256] + (product[8:16, 0:256] + product[0:8, 256:512])
    out[...] = scaled[0:4] / math.sqrt(FEATS)

    wait(all_first.at[pl.ds(0, 7)], mom_sem.at[0, 0])
    wait(all_second.at[pl.ds(0, 7)], mom_sem.at[0, 1])
    wait(all_proj.at[pl.ds(0, 7)], proj_sem.at[0, 0])
    for k in range(GROUPS):
        wait(all_rows.at[k, pl.ds(0, 7)], row_sem.at[0, k])
        wait(from_core.at[k], core_sem.at[0, k])
        wait(from_y.at[k], y_sem.at[0, k])
        wait(from_xz.at[k], xz_sem.at[0, k])
    wait(unit.at[pl.ds(0, 240)], unit_sem.at[0, 0])
    wait(unit.at[pl.ds(0, 768)], unit_sem.at[0, 1])
    wait(unit.at[pl.ds(0, 1024)], unit_sem.at[0, 2])


def per_device(train, target, proj, first, second, owners):
    vmem = pltpu.VMEM
    dma = pltpu.SemaphoreType.DMA
    anywhere = pl.BlockSpec(memory_space=pl.ANY)
    return pl.pallas_call(
        kernel,
        out_shape=jax.ShapeDtypeStruct((4, 256), F32),
        in_specs=[anywhere] * 5 + [pl.BlockSpec(memory_space=pltpu.SMEM)],
        out_specs=pl.BlockSpec(memory_space=pltpu.VMEM),
        scratch_shapes=[
            vmem((64, 16384), BF16),
            vmem((32, 16384), BF16),
            vmem((64, 16384), BF16),
            vmem((32, 16384), BF16),
            vmem((8, 128, COLS), BF16),
            vmem((GROUPS, 8, 16, COLS), BF16),
            vmem((8, 1, COLS), F32),
            vmem((8, 1, COLS), F32),
            vmem((8, 16, COLS), BF16),
            vmem((128, COLS), BF16),
            vmem((GROUPS, 128, FEATS), F32),
            vmem((GROUPS, 64, FEATS), F32),
            vmem((GROUPS, 64, FEATS), F32),
            vmem((GROUPS, 3, 16, FEATS), F32),
            vmem((GROUPS, 128, 128), F32),
            vmem((GROUPS, 120, 128), F32),
            vmem((2048, 128), F32),
            vmem((512, FEATS), BF16),
            vmem((64, 128), F32),
            dma((2,)),
            dma((2, 2)),
            dma((2, 1)),
            dma((2, GROUPS)),
            dma((2, GROUPS)),
            dma((2, GROUPS)),
            dma((2, GROUPS)),
            dma((2, 3)),
        ],
        compiler_params=pltpu.CompilerParams(
            collective_id=0, has_side_effects=True, vmem_limit_bytes=60 * 2**20
        ),
    )(train, target, proj, first, second, owners)


def solution(mesh):
    placed = (
        P("dp", "param"),
        P("dp", "param"),
        P("dp", "param"),
        P("param", "dp", None),
        P("param", "dp", None),
        P("param", None),
    )
    return jax.shard_map(
        per_device, mesh=mesh, in_specs=placed, out_specs=P(("dp", "param"), None), check_vma=False
    )
```

```python
import math

import jax
import jax.numpy as jnp
from jax import lax
from jax.experimental import pallas as pl
from jax.experimental.pallas import tpu as pltpu
from jax.sharding import PartitionSpec as P

MESH = pl.DeviceIdType.MESH
F32, BF16 = jnp.float32, jnp.bfloat16
COLS = 2048
FEATS = 1024
HALF = 512
DEPTH = COLS // 2
PIECES = 8
GROUPS = 4
FAR_FIRST = (2, 6, 5, 7, 1, 3, 4)


def one_hot(rows, source_of, along=0):
    r = lax.broadcasted_iota(jnp.int32, (rows, rows), along)
    s = lax.broadcasted_iota(jnp.int32, (rows, rows), 1 - along)
    return jnp.where(source_of(r) == s, 1.0, 0.0).astype(BF16)


def bits(r, low, width):
    return (r >> low) & ((1 << width) - 1)


def kernel(
    train, target, proj, first, second, owners,
    out,
    raw_rows, sorted_rows, all_targets, all_proj, columns_of, all_rows, all_first, all_second,
    target_lhs, mixed, lhs,
    target_part, target_from_core, target_by_y, target_from_y,
    part, from_core, by_y, from_y, by_xz, from_xz, raw_unit, unit_cat, own_rows,
    load_sem, mom_sem, target_sem, proj_sem, row_sem, core_sem, y_sem, xz_sem, gather_sem,
):
    dp = lax.axis_index("dp")
    param = lax.axis_index("param")
    x_hi, y, core = param // 8, (param // 2) % 4, param % 2
    place = x_hi * 8 + dp

    def dp_peer(o):
        return (dp + o) % 8, {"dp": (dp + o) % 8, "param": param}

    core_peer = {"dp": dp, "param": x_hi * 8 + y * 2 + (1 - core)}

    def y_peer(o):
        other = (y + o) % 4
        return other, {"dp": dp, "param": x_hi * 8 + other * 2 + core}

    def xz_peer(o):
        far, near = (x_hi + o // 8) % 2, (dp + o % 8) % 8
        return far * 8 + near, {"dp": near, "param": far * 8 + y * 2 + core}

    def send(src, dst, sems, at, device):
        pltpu.make_async_remote_copy(
            src_ref=src, dst_ref=dst, send_sem=sems.at[0, at], recv_sem=sems.at[1, at],
            device_id=device, device_id_type=MESH,
        ).start()

    def keep(src, dst, sem):
        pltpu.make_async_copy(src, dst, sem).start()

    def wait(ref, sem):
        pltpu.make_async_copy(ref, ref, sem).wait()

    def columns(owner):
        return pl.ds(owner * COLS, COLS)

    keep(train, raw_rows, load_sem.at[0])
    barrier = pltpu.get_barrier_semaphore()
    peers = [xz_peer(o)[1] for o in range(1, 16)] + [core_peer] + [y_peer(o)[1] for o in range(1, 4)]
    for device in peers:
        pl.semaphore_signal(barrier, inc=1, device_id=device, device_id_type=MESH)
    pl.semaphore_wait(barrier, len(peers))

    def send_targets():
        for o in FAR_FIRST:
            other, device = dp_peer(o)
            send(target.at[:, columns(other)], all_targets.at[dp], target_sem, 0, device)
        keep(target.at[:, columns(dp)], all_targets.at[dp], target_sem.at[1, 0])

    def send_proj(i):
        rows = pl.ds(i * 16, 16)
        for o in FAR_FIRST:
            other, device = dp_peer(o)
            send(proj.at[rows, columns(other)], all_proj.at[i, dp], proj_sem, i, device)
        keep(proj.at[rows, columns(dp)], all_proj.at[i, dp], proj_sem.at[1, i])

    def send_moments():
        for o in FAR_FIRST:
            other, device = dp_peer(o)
            send(first.at[0], all_first.at[dp], mom_sem, 0, device)
            send(second.at[0], all_second.at[dp], mom_sem, 1, device)
        keep(first.at[0], all_first.at[dp], mom_sem.at[1, 0])
        keep(second.at[0], all_second.at[dp], mom_sem.at[1, 1])

    def send_rows(k, half):
        rows, at = pl.ds(k * 16, 16), k * 2 + half

        def some(owner):
            return sorted_rows.at[rows, pl.ds(owner * COLS + half * DEPTH, DEPTH)]

        for o in FAR_FIRST:
            other, device = dp_peer(o)
            send(some(other), all_rows.at[at, dp], row_sem, at, device)
        keep(some(dp), all_rows.at[at, dp], row_sem.at[1, at])

    def sort_rows():
        wait(raw_rows, load_sem.at[0])
        pick = one_hot(64, lambda r: (r & 15) * 4 + (r >> 4))

        @pl.loop(0, 16)
        def _(t):
            cols = pl.ds(pl.multiple_of(t * 1024, 1024), 1024)
            sorted_rows[:, cols] = jnp.dot(
                pick, raw_rows[:, cols], preferred_element_type=F32
            ).astype(BF16)

    def regroup_targets():
        wait(all_targets, target_sem.at[1, 0])
        regroup = one_hot(
            256,
            lambda r: bits(r, 1, 3) * 32 + bits(r, 4, 1) * 16 + bits(r, 5, 2) * 4
            + bits(r, 7, 1) * 2 + bits(r, 0, 1),
        )

        @pl.loop(0, 8)
        def _(t):
            cols = pl.ds(pl.multiple_of(t * 256, 256), 256)
            target_lhs[:, cols] = jnp.dot(
                regroup, all_targets[:, :, cols].reshape(256, 256), preferred_element_type=F32
            ).astype(BF16)

    def transpose(i):
        wait(all_proj.at[i], proj_sem.at[1, i])
        same = one_hot(256, lambda r: r)
        for t in range(8):
            at = slice(t * 256, (t + 1) * 256)
            columns_of[at, i * 128 : (i + 1) * 128] = lax.dot_general(
                same, all_proj[i, :, :, at].reshape(128, 256), (((1,), (1,)), ((), ())),
                preferred_element_type=F32,
            ).astype(BF16)

    def multiply_targets(h):
        target_part[h] = jnp.dot(
            target_lhs[...], columns_of[:, h * HALF : (h + 1) * HALF], preferred_element_type=F32
        )
        away = pl.ds((1 - core) * 128, 128)
        send(target_part.at[h, away], target_from_core.at[h], core_sem, h, core_peer)

    def multiply(k, half):
        at = k * 2 + half
        wait(all_rows.at[at], row_sem.at[1, at])

        @pl.loop(0, 8)
        def _(s):
            for t in range(2):
                cols = slice(t * 512, (t + 1) * 512)
                own = slice(half * DEPTH + t * 512, half * DEPTH + (t + 1) * 512)
                g = all_rows[at, s, :, cols].astype(F32)
                upper = first_row[:, own] + 0.1 * g
                lower = jnp.sqrt(second_row[:, own] + 0.001 * g * g) + 1e-08
                mixed[s, :, cols] = (upper / lower).astype(BF16)

        for t in range(2):
            cols = slice(t * 512, (t + 1) * 512)
            lhs[:, cols] = jnp.dot(
                regroup, mixed[:, :, cols].reshape(128, 512), preferred_element_type=F32
            ).astype(BF16)
        done = jnp.dot(
            lhs[...], columns_of[half * DEPTH : (half + 1) * DEPTH], preferred_element_type=F32
        )
        if half == 0:
            part[k] = done
        else:
            part[k] = part[k] + done
            away = pl.ds((1 - core) * 64, 64)
            send(part.at[k, away], from_core.at[k], core_sem, 2 + k, core_peer)

    def add_core(g):
        if g < 2:
            here, there, total, arrived, k, rows = (
                target_part, target_from_core, target_by_y, target_from_y, g, 32,
            )
        else:
            here, there, total, arrived, k, rows = part, from_core, by_y, from_y, g - 2, 16
        wait(there.at[k], core_sem.at[1, g])

        @pl.loop(0, 4)
        def _(t):
            at = pl.ds(t * rows, rows)
            total[k, at] = here[k, pl.ds((core * 4 + t) * rows, rows)] + there[k, at]

        for o in (2, 1, 3):
            other, device = y_peer(o)
            send(total.at[k, pl.ds(other * rows, rows)], arrived.at[k, o - 1], y_sem, g, device)

    def add_y(g):
        if g < 2:
            total, arrived, k, rows = target_by_y, target_from_y, g, 32
        else:
            total, arrived, k, rows = by_y, from_y, g - 2, 16
        wait(arrived.at[k], y_sem.at[1, g])
        done = total[k, pl.ds(y * rows, rows)] + arrived[k, 0] + arrived[k, 1] + arrived[k, 2]
        tiles = 128 // rows
        for s in range(tiles):
            by_xz[g, pl.ds(s, rows, stride=tiles), :] = done[:, s * 128 : (s + 1) * 128]
        for o in range(1, 16):
            other, device = xz_peer(o)
            send(by_xz.at[g, pl.ds(other * 8, 8)], from_xz.at[g, pl.ds(o * 8 - 8, 8)], xz_sem, g, device)

    def add_xz(g):
        wait(from_xz.at[g], xz_sem.at[1, g])
        f = by_xz[g, pl.ds(place * 8, 8)]
        for o in range(15):
            f = f + from_xz[g, o * 8 : o * 8 + 8]
        return f

    spot = (core * 4 + y) * 16 + place

    def gather_xz(h):
        mine = raw_unit.at[h, pl.ds(spot * 8, 8)]
        raw_unit[h, pl.ds(spot * 8, 8)] = add_xz(h)
        for o in range(1, 16):
            send(mine, mine, gather_sem, h * 3, xz_peer(o)[1])

    def gather_y(h):
        wait(raw_unit.at[h, pl.ds(0, 120)], gather_sem.at[1, h * 3])
        mine = raw_unit.at[h, pl.ds((core * 4 + y) * 128, 128)]
        for o in (2, 1, 3):
            send(mine, mine, gather_sem, h * 3 + 1, y_peer(o)[1])

    def gather_core(h):
        wait(raw_unit.at[h, pl.ds(0, 384)], gather_sem.at[1, h * 3 + 1])
        mine = raw_unit.at[h, pl.ds(core * 512, 512)]
        send(mine, mine, gather_sem, h * 3 + 2, core_peer)

    def arrange():
        for h in range(2):
            wait(raw_unit.at[h, pl.ds(0, 512)], gather_sem.at[1, h * 3 + 2])
        natural = one_hot(
            256,
            lambda r: bits(r, 0, 1) * 128 + bits(r, 1, 1) * 64 + bits(r, 2, 2) * 16
            + bits(r, 4, 1) * 8 + bits(r, 5, 3),
            along=1,
        )

        def piece(h, s, c):
            return raw_unit[h, pl.ds(c * 4 + s, 128, stride=8), :]

        scale = []
        for c in range(2):
            squares = jnp.zeros((128, 128), F32)
            for h in range(2):
                for s in range(4):
                    f = piece(h, s, c)
                    squares = squares + f * f
            mean = jnp.sum(squares, axis=1, keepdims=True) / FEATS
            scale.append(lax.rsqrt(mean + 1e-06))
        for h in range(2):
            for s in range(4):
                f = jnp.concatenate([(piece(h, s, c) * scale[c]).T for c in range(2)], axis=1)
                high = f.astype(BF16)
                low = (f - high.astype(F32)).astype(BF16)
                at = slice(h * HALF + s * 128, h * HALF + (s + 1) * 128)
                unit_cat[at, 0:256] = jnp.dot(high, natural, preferred_element_type=F32).astype(BF16)
                unit_cat[at, 256:512] = jnp.dot(low, natural, preferred_element_type=F32).astype(BF16)

    def train_row(g):
        f = add_xz(g)
        mean = jnp.sum(f * f, keepdims=True) / FEATS
        own_rows[(g - 2) * 8 : (g - 1) * 8] = f * lax.rsqrt(mean + 1e-06)

    send_targets()
    send_proj(0)
    send_moments()
    send_proj(1)
    own_rows[...] = jnp.zeros_like(own_rows)
    sort_rows()
    regroup_targets()
    send_proj(2)
    transpose(0)
    send_proj(3)
    transpose(1)
    send_proj(4)
    wait(all_first, mom_sem.at[1, 0])
    wait(all_second, mom_sem.at[1, 1])
    owner = owners[0, dp]
    first_row = 0.9 * all_first[owner]
    second_row = 0.999 * all_second[owner]
    regroup = one_hot(
        128, lambda r: bits(r, 0, 3) * 16 + bits(r, 3, 1) * 8 + bits(r, 4, 2) * 2 + bits(r, 6, 1)
    )

    transpose(2)
    send_proj(5)
    transpose(3)
    multiply_targets(0)
    send_proj(6)
    add_core(0)
    transpose(4)
    send_proj(7)
    transpose(5)
    add_y(0)
    send_rows(0, 0)
    send_rows(0, 1)
    transpose(6)
    send_rows(1, 0)
    transpose(7)
    multiply_targets(1)
    gather_xz(0)
    send_rows(1, 1)
    add_core(1)
    multiply(0, 0)
    multiply(0, 1)
    add_y(1)
    send_rows(2, 0)
    gather_y(0)
    send_rows(2, 1)
    add_core(2)
    multiply(1, 0)
    multiply(1, 1)
    gather_xz(1)
    send_rows(3, 0)
    send_rows(3, 1)
    add_core(3)
    add_y(2)
    gather_core(0)
    multiply(2, 0)
    multiply(2, 1)
    gather_y(1)
    add_y(3)
    add_core(4)
    multiply(3, 0)
    multiply(3, 1)
    gather_core(1)
    add_core(5)
    train_row(2)
    add_y(4)
    train_row(3)
    arrange()
    train_row(4)
    add_y(5)
    train_row(5)

    rows = jnp.concatenate([own_rows[pl.ds(s, 8, stride=8), :] for s in range(8)], axis=1)
    high = rows.astype(BF16)
    low = (rows - high.astype(F32)).astype(BF16)
    product = jnp.dot(
        jnp.concatenate([high, low], axis=0), unit_cat[...], preferred_element_type=F32
    )
    scaled = product[0:8, 0:256] + (product[8:16, 0:256] + product[0:8, 256:512])
    out[...] = scaled[0:4] / math.sqrt(FEATS)

    wait(all_targets.at[pl.ds(0, 7)], target_sem.at[0, 0])
    wait(all_first.at[pl.ds(0, 7)], mom_sem.at[0, 0])
    wait(all_second.at[pl.ds(0, 7)], mom_sem.at[0, 1])
    for i in range(PIECES):
        wait(all_proj.at[i, pl.ds(0, 7)], proj_sem.at[0, i])
    for h in range(2):
        wait(target_from_core.at[h], core_sem.at[0, h])
        wait(target_from_y.at[h], y_sem.at[0, h])
        wait(from_xz.at[h], xz_sem.at[0, h])
        wait(raw_unit.at[h, pl.ds(0, 120)], gather_sem.at[0, h * 3])
        wait(raw_unit.at[h, pl.ds(0, 384)], gather_sem.at[0, h * 3 + 1])
        wait(raw_unit.at[h, pl.ds(0, 512)], gather_sem.at[0, h * 3 + 2])
    for at in range(GROUPS * 2):
        wait(all_rows.at[at, pl.ds(0, 7)], row_sem.at[0, at])
    for k in range(GROUPS):
        wait(from_core.at[k], core_sem.at[0, 2 + k])
        wait(from_y.at[k], y_sem.at[0, 2 + k])
        wait(from_xz.at[2 + k], xz_sem.at[0, 2 + k])


def per_device(train, target, proj, first, second, owners):
    vmem = pltpu.VMEM
    dma = pltpu.SemaphoreType.DMA
    anywhere = pl.BlockSpec(memory_space=pl.ANY)
    return pl.pallas_call(
        kernel,
        out_shape=jax.ShapeDtypeStruct((4, 256), F32),
        in_specs=[anywhere] * 5 + [pl.BlockSpec(memory_space=pltpu.SMEM)],
        out_specs=pl.BlockSpec(memory_space=pltpu.VMEM),
        scratch_shapes=[
            vmem((64, 16384), BF16),
            vmem((64, 16384), BF16),
            vmem((8, 32, COLS), BF16),
            vmem((PIECES, 8, 16, COLS), BF16),
            vmem((COLS, FEATS), BF16),
            vmem((GROUPS * 2, 8, 16, DEPTH), BF16),
            vmem((8, 1, COLS), F32),
            vmem((8, 1, COLS), F32),
            vmem((256, COLS), BF16),
            vmem((8, 16, DEPTH), BF16),
            vmem((128, DEPTH), BF16),
            vmem((2, 256, HALF), F32),
            vmem((2, 128, HALF), F32),
            vmem((2, 128, HALF), F32),
            vmem((2, 3, 32, HALF), F32),
            vmem((GROUPS, 128, FEATS), F32),
            vmem((GROUPS, 64, FEATS), F32),
            vmem((GROUPS, 64, FEATS), F32),
            vmem((GROUPS, 3, 16, FEATS), F32),
            vmem((2 + GROUPS, 128, 128), F32),
            vmem((2 + GROUPS, 120, 128), F32),
            vmem((2, 1024, 128), F32),
            vmem((FEATS, 512), BF16),
            vmem((64, 128), F32),
            dma((1,)),
            dma((2, 2)),
            dma((2, 1)),
            dma((2, PIECES)),
            dma((2, GROUPS * 2)),
            dma((2, 2 + GROUPS)),
            dma((2, 2 + GROUPS)),
            dma((2, 2 + GROUPS)),
            dma((2, 6)),
        ],
        compiler_params=pltpu.CompilerParams(
            collective_id=0, has_side_effects=True, vmem_limit_bytes=60 * 2**20
        ),
    )(train, target, proj, first, second, owners)


def solution(mesh):
    placed = (
        P("dp", "param"),
        P("dp", "param"),
        P("dp", "param"),
        P("param", "dp", None),
        P("param", "dp", None),
        P("param", None),
    )
    return jax.shard_map(
        per_device, mesh=mesh, in_specs=placed, out_specs=P(("dp", "param"), None), check_vma=False
    )
```

```python
import math

import jax
import jax.numpy as jnp
from jax import lax
from jax.experimental import pallas as pl
from jax.experimental.pallas import tpu as pltpu
from jax.sharding import PartitionSpec as P

MESH = pl.DeviceIdType.MESH
F32, BF16 = jnp.float32, jnp.bfloat16
COLS = 2048
FEATS = 1024
HALF = 512
DEPTH = COLS // 2
PIECES = 8
GROUPS = 4
LAST = GROUPS - 1
FAR_FIRST = (2, 6, 5, 7, 1, 3, 4)
XZ_FAR_FIRST = (10, 14, 13, 15, 9, 11, 12, 2, 6, 8, 5, 7, 1, 3, 4)


def one_hot(rows, source_of, along=0):
    r = lax.broadcasted_iota(jnp.int32, (rows, rows), along)
    s = lax.broadcasted_iota(jnp.int32, (rows, rows), 1 - along)
    return jnp.where(source_of(r) == s, 1.0, 0.0).astype(BF16)


def bits(r, low, width):
    return (r >> low) & ((1 << width) - 1)


def kernel(
    train, target, proj, first, second, owners,
    out,
    raw_rows, sorted_rows, all_targets, all_proj, columns_of, all_rows, all_first, all_second,
    target_lhs, mixed, lhs,
    target_part, target_from_core, target_by_y, target_from_y,
    part, from_core, by_y, from_y, last_part, last_from_core, last_by_y, last_from_y, by_xz, from_xz, raw_unit, unit_cat, own_rows,
    load_sem, mom_sem, target_sem, proj_sem, row_sem, core_sem, y_sem, xz_sem, gather_sem,
):
    dp = lax.axis_index("dp")
    param = lax.axis_index("param")
    x_hi, y, core = param // 8, (param // 2) % 4, param % 2
    place = x_hi * 8 + dp

    def dp_peer(o):
        return (dp + o) % 8, {"dp": (dp + o) % 8, "param": param}

    core_peer = {"dp": dp, "param": x_hi * 8 + y * 2 + (1 - core)}

    def y_peer(o):
        other = (y + o) % 4
        return other, {"dp": dp, "param": x_hi * 8 + other * 2 + core}

    def xz_peer(o):
        far, near = (x_hi + o // 8) % 2, (dp + o % 8) % 8
        return far * 8 + near, {"dp": near, "param": far * 8 + y * 2 + core}

    def send(src, dst, sems, at, device):
        pltpu.make_async_remote_copy(
            src_ref=src, dst_ref=dst, send_sem=sems.at[0, at], recv_sem=sems.at[1, at],
            device_id=device, device_id_type=MESH,
        ).start()

    def keep(src, dst, sem):
        pltpu.make_async_copy(src, dst, sem).start()

    def wait(ref, sem):
        pltpu.make_async_copy(ref, ref, sem).wait()

    def columns(owner):
        return pl.ds(owner * COLS, COLS)

    keep(train, raw_rows, load_sem.at[0])
    barrier = pltpu.get_barrier_semaphore()
    peers = [xz_peer(o)[1] for o in range(1, 16)] + [core_peer] + [y_peer(o)[1] for o in range(1, 4)]
    for device in peers:
        pl.semaphore_signal(barrier, inc=1, device_id=device, device_id_type=MESH)
    pl.semaphore_wait(barrier, len(peers))

    def send_targets():
        for o in FAR_FIRST:
            other, device = dp_peer(o)
            send(target.at[:, columns(other)], all_targets.at[dp], target_sem, 0, device)
        keep(target.at[:, columns(dp)], all_targets.at[dp], target_sem.at[1, 0])

    def send_proj(i):
        rows = pl.ds(i * 16, 16)
        for o in FAR_FIRST:
            other, device = dp_peer(o)
            send(proj.at[rows, columns(other)], all_proj.at[i, dp], proj_sem, i, device)
        keep(proj.at[rows, columns(dp)], all_proj.at[i, dp], proj_sem.at[1, i])

    def send_moments():
        for o in FAR_FIRST:
            other, device = dp_peer(o)
            send(first.at[0], all_first.at[dp], mom_sem, 0, device)
            send(second.at[0], all_second.at[dp], mom_sem, 1, device)
        keep(first.at[0], all_first.at[dp], mom_sem.at[1, 0])
        keep(second.at[0], all_second.at[dp], mom_sem.at[1, 1])

    def send_rows(k, half):
        rows, at = pl.ds(k * 16, 16), k * 2 + half

        def some(owner):
            return sorted_rows.at[rows, pl.ds(owner * COLS + half * DEPTH, DEPTH)]

        for o in FAR_FIRST:
            other, device = dp_peer(o)
            send(some(other), all_rows.at[at, dp], row_sem, at, device)
        keep(some(dp), all_rows.at[at, dp], row_sem.at[1, at])

    def sort_rows():
        wait(raw_rows, load_sem.at[0])
        pick = one_hot(64, lambda r: (r & 15) * 4 + (r >> 4))

        @pl.loop(0, 16)
        def _(t):
            cols = pl.ds(pl.multiple_of(t * 1024, 1024), 1024)
            sorted_rows[:, cols] = jnp.dot(
                pick, raw_rows[:, cols], preferred_element_type=F32
            ).astype(BF16)

    def regroup_targets():
        wait(all_targets, target_sem.at[1, 0])
        regroup = one_hot(
            256,
            lambda r: bits(r, 1, 3) * 32 + bits(r, 4, 1) * 16 + bits(r, 5, 2) * 4
            + bits(r, 7, 1) * 2 + bits(r, 0, 1),
        )

        @pl.loop(0, 8)
        def _(t):
            cols = pl.ds(pl.multiple_of(t * 256, 256), 256)
            target_lhs[:, cols] = jnp.dot(
                regroup, all_targets[:, :, cols].reshape(256, 256), preferred_element_type=F32
            ).astype(BF16)

    def transpose(i):
        wait(all_proj.at[i], proj_sem.at[1, i])
        same = one_hot(256, lambda r: r)
        for t in range(8):
            at = slice(t * 256, (t + 1) * 256)
            columns_of[at, i * 128 : (i + 1) * 128] = lax.dot_general(
                same, all_proj[i, :, :, at].reshape(128, 256), (((1,), (1,)), ((), ())),
                preferred_element_type=F32,
            ).astype(BF16)

    def multiply_targets(h):
        target_part[h] = jnp.dot(
            target_lhs[...], columns_of[:, h * HALF : (h + 1) * HALF], preferred_element_type=F32
        )
        away = pl.ds((1 - core) * 128, 128)
        send(target_part.at[h, away], target_from_core.at[h], core_sem, h, core_peer)

    def multiply(k, half):
        at = k * 2 + half
        wait(all_rows.at[at], row_sem.at[1, at])

        @pl.loop(0, 8)
        def _(s):
            for t in range(2):
                cols = slice(t * 512, (t + 1) * 512)
                own = slice(half * DEPTH + t * 512, half * DEPTH + (t + 1) * 512)
                g = all_rows[at, s, :, cols].astype(F32)
                upper = first_row[:, own] + 0.1 * g
                lower = jnp.sqrt(second_row[:, own] + 0.001 * g * g) + 1e-08
                mixed[s, :, cols] = (upper / lower).astype(BF16)

        for t in range(2):
            cols = slice(t * 512, (t + 1) * 512)
            lhs[:, cols] = jnp.dot(
                regroup, mixed[:, :, cols].reshape(128, 512), preferred_element_type=F32
            ).astype(BF16)
        done = jnp.dot(
            lhs[...], columns_of[half * DEPTH : (half + 1) * DEPTH], preferred_element_type=F32
        )
        if half == 0:
            part[k] = done
        else:
            part[k] = part[k] + done
            away = pl.ds((1 - core) * 64, 64)
            if k == LAST:
                last_part[...] = part[k, away].astype(BF16)
                send(last_part, last_from_core, core_sem, 2 + k, core_peer)
            else:
                send(part.at[k, away], from_core.at[k], core_sem, 2 + k, core_peer)

    def add_core(g):
        if g < 2:
            here, there, total, arrived, k, rows = (
                target_part, target_from_core, target_by_y, target_from_y, g, 32,
            )
        else:
            here, there, total, arrived, k, rows = part, from_core, by_y, from_y, g - 2, 16
        wait(there.at[k], core_sem.at[1, g])

        @pl.loop(0, 4)
        def _(t):
            at = pl.ds(t * rows, rows)
            total[k, at] = here[k, pl.ds((core * 4 + t) * rows, rows)] + there[k, at]

        for o in (2, 1, 3):
            other, device = y_peer(o)
            send(total.at[k, pl.ds(other * rows, rows)], arrived.at[k, o - 1], y_sem, g, device)

    def add_core_last():
        wait(last_from_core, core_sem.at[1, 5])
        total = part[LAST, pl.ds(core * 64, 64)] + last_from_core[...].astype(F32)
        by_y[LAST] = total
        last_by_y[...] = total.astype(BF16)
        for o in (2, 1, 3):
            other, device = y_peer(o)
            send(last_by_y.at[pl.ds(other * 16, 16)], last_from_y.at[o - 1], y_sem, 5, device)

    def add_y(g):
        if g == 5:
            wait(last_from_y, y_sem.at[1, g])
            total, k, rows = by_y, LAST, 16
        elif g < 2:
            total, arrived, k, rows = target_by_y, target_from_y, g, 32
        else:
            total, arrived, k, rows = by_y, from_y, g - 2, 16
        done = total[k, pl.ds(y * rows, rows)]
        if g < 5:
            wait(arrived.at[k], y_sem.at[1, g])
            done = done + arrived[k, 0] + arrived[k, 1] + arrived[k, 2]
        else:
            for o in range(3):
                done = done + last_from_y[o].astype(F32)
        tiles = 128 // rows
        for s in range(tiles):
            by_xz[g, pl.ds(s, rows, stride=tiles), :] = done[:, s * 128 : (s + 1) * 128]
        for o in XZ_FAR_FIRST:
            other, device = xz_peer(o)
            send(by_xz.at[g, pl.ds(other * 8, 8)], from_xz.at[g, pl.ds(o * 8 - 8, 8)], xz_sem, g, device)

    def add_xz(g):
        wait(from_xz.at[g], xz_sem.at[1, g])
        f = by_xz[g, pl.ds(place * 8, 8)]
        for o in range(15):
            f = f + from_xz[g, o * 8 : o * 8 + 8]
        return f

    spot = (core * 4 + y) * 16 + place

    def gather_xz(h):
        mine = raw_unit.at[h, pl.ds(spot * 8, 8)]
        raw_unit[h, pl.ds(spot * 8, 8)] = add_xz(h)
        for o in XZ_FAR_FIRST:
            send(mine, mine, gather_sem, h * 3, xz_peer(o)[1])

    def gather_y(h):
        wait(raw_unit.at[h, pl.ds(0, 120)], gather_sem.at[1, h * 3])
        mine = raw_unit.at[h, pl.ds((core * 4 + y) * 128, 128)]
        for o in (2, 1, 3):
            send(mine, mine, gather_sem, h * 3 + 1, y_peer(o)[1])

    def gather_core(h):
        wait(raw_unit.at[h, pl.ds(0, 384)], gather_sem.at[1, h * 3 + 1])
        mine = raw_unit.at[h, pl.ds(core * 512, 512)]
        send(mine, mine, gather_sem, h * 3 + 2, core_peer)

    def arrange():
        for h in range(2):
            wait(raw_unit.at[h, pl.ds(0, 512)], gather_sem.at[1, h * 3 + 2])
        natural = one_hot(
            256,
            lambda r: bits(r, 0, 1) * 128 + bits(r, 1, 1) * 64 + bits(r, 2, 2) * 16
            + bits(r, 4, 1) * 8 + bits(r, 5, 3),
            along=1,
        )

        def piece(h, s, c):
            return raw_unit[h, pl.ds(c * 4 + s, 128, stride=8), :]

        scale = []
        for c in range(2):
            squares = jnp.zeros((128, 128), F32)
            for h in range(2):
                for s in range(4):
                    f = piece(h, s, c)
                    squares = squares + f * f
            mean = jnp.sum(squares, axis=1, keepdims=True) / FEATS
            scale.append(lax.rsqrt(mean + 1e-06))
        for h in range(2):
            for s in range(4):
                f = jnp.concatenate([(piece(h, s, c) * scale[c]).T for c in range(2)], axis=1)
                high = f.astype(BF16)
                low = (f - high.astype(F32)).astype(BF16)
                at = slice(h * HALF + s * 128, h * HALF + (s + 1) * 128)
                unit_cat[at, 0:256] = jnp.dot(high, natural, preferred_element_type=F32).astype(BF16)
                unit_cat[at, 256:512] = jnp.dot(low, natural, preferred_element_type=F32).astype(BF16)

    def train_row(g):
        f = add_xz(g)
        mean = jnp.sum(f * f, keepdims=True) / FEATS
        own_rows[(g - 2) * 8 : (g - 1) * 8] = f * lax.rsqrt(mean + 1e-06)

    def sent():
        wait(all_targets.at[pl.ds(0, 7)], target_sem.at[0, 0])
        wait(all_first.at[pl.ds(0, 7)], mom_sem.at[0, 0])
        wait(all_second.at[pl.ds(0, 7)], mom_sem.at[0, 1])
        for i in range(PIECES):
            wait(all_proj.at[i, pl.ds(0, 7)], proj_sem.at[0, i])
        for h in range(2):
            wait(target_from_core.at[h], core_sem.at[0, h])
            wait(target_from_y.at[h], y_sem.at[0, h])
            wait(from_xz.at[h], xz_sem.at[0, h])
            wait(raw_unit.at[h, pl.ds(0, 120)], gather_sem.at[0, h * 3])
            wait(raw_unit.at[h, pl.ds(0, 384)], gather_sem.at[0, h * 3 + 1])
            wait(raw_unit.at[h, pl.ds(0, 512)], gather_sem.at[0, h * 3 + 2])
        for at in range(GROUPS * 2):
            wait(all_rows.at[at, pl.ds(0, 7)], row_sem.at[0, at])
        for k in range(GROUPS):
            wait(last_from_core if k == LAST else from_core.at[k], core_sem.at[0, 2 + k])
            wait(last_from_y if k == LAST else from_y.at[k], y_sem.at[0, 2 + k])
            if k != LAST:
                wait(from_xz.at[2 + k], xz_sem.at[0, 2 + k])

    send_targets()
    send_proj(0)
    send_moments()
    send_proj(1)
    own_rows[...] = jnp.zeros_like(own_rows)
    sort_rows()
    regroup_targets()
    send_proj(2)
    transpose(0)
    send_proj(3)
    transpose(1)
    send_proj(4)
    wait(all_first, mom_sem.at[1, 0])
    wait(all_second, mom_sem.at[1, 1])
    owner = owners[0, dp]
    first_row = 0.9 * all_first[owner]
    second_row = 0.999 * all_second[owner]
    regroup = one_hot(
        128, lambda r: bits(r, 0, 3) * 16 + bits(r, 3, 1) * 8 + bits(r, 4, 2) * 2 + bits(r, 6, 1)
    )

    transpose(2)
    send_proj(5)
    transpose(3)
    multiply_targets(0)
    send_proj(6)
    add_core(0)
    transpose(4)
    send_proj(7)
    transpose(5)
    add_y(0)
    send_rows(0, 0)
    send_rows(0, 1)
    transpose(6)
    send_rows(1, 0)
    transpose(7)
    multiply_targets(1)
    gather_xz(0)
    send_rows(1, 1)
    add_core(1)
    multiply(0, 0)
    multiply(0, 1)
    add_y(1)
    send_rows(2, 0)
    gather_y(0)
    send_rows(2, 1)
    add_core(2)
    multiply(1, 0)
    multiply(1, 1)
    gather_xz(1)
    send_rows(3, 0)
    send_rows(3, 1)
    add_core(3)
    add_y(2)
    gather_core(0)
    multiply(2, 0)
    multiply(2, 1)
    gather_y(1)
    add_y(3)
    add_core(4)
    multiply(3, 0)
    multiply(3, 1)
    add_core_last()
    gather_core(1)
    add_y(4)
    train_row(2)
    train_row(3)
    arrange()
    add_y(5)
    sent()
    train_row(4)
    train_row(5)

    rows = jnp.concatenate([own_rows[pl.ds(s, 8, stride=8), :] for s in range(8)], axis=1)
    high = rows.astype(BF16)
    low = (rows - high.astype(F32)).astype(BF16)
    product = jnp.dot(
        jnp.concatenate([high, low], axis=0), unit_cat[...], preferred_element_type=F32
    )
    scaled = product[0:8, 0:256] + (product[8:16, 0:256] + product[0:8, 256:512])
    out[...] = scaled[0:4] / math.sqrt(FEATS)

    wait(from_xz.at[5], xz_sem.at[0, 5])


def per_device(train, target, proj, first, second, owners):
    vmem = pltpu.VMEM
    dma = pltpu.SemaphoreType.DMA
    anywhere = pl.BlockSpec(memory_space=pl.ANY)
    return pl.pallas_call(
        kernel,
        out_shape=jax.ShapeDtypeStruct((4, 256), F32),
        in_specs=[anywhere] * 5 + [pl.BlockSpec(memory_space=pltpu.SMEM)],
        out_specs=pl.BlockSpec(memory_space=pltpu.VMEM),
        scratch_shapes=[
            vmem((64, 16384), BF16),
            vmem((64, 16384), BF16),
            vmem((8, 32, COLS), BF16),
            vmem((PIECES, 8, 16, COLS), BF16),
            vmem((COLS, FEATS), BF16),
            vmem((GROUPS * 2, 8, 16, DEPTH), BF16),
            vmem((8, 1, COLS), F32),
            vmem((8, 1, COLS), F32),
            vmem((256, COLS), BF16),
            vmem((8, 16, DEPTH), BF16),
            vmem((128, DEPTH), BF16),
            vmem((2, 256, HALF), F32),
            vmem((2, 128, HALF), F32),
            vmem((2, 128, HALF), F32),
            vmem((2, 3, 32, HALF), F32),
            vmem((GROUPS, 128, FEATS), F32),
            vmem((LAST, 64, FEATS), F32),
            vmem((GROUPS, 64, FEATS), F32),
            vmem((LAST, 3, 16, FEATS), F32),
            vmem((64, FEATS), BF16),
            vmem((64, FEATS), BF16),
            vmem((64, FEATS), BF16),
            vmem((3, 16, FEATS), BF16),
            vmem((2 + GROUPS, 128, 128), F32),
            vmem((2 + GROUPS, 120, 128), F32),
            vmem((2, 1024, 128), F32),
            vmem((FEATS, 512), BF16),
            vmem((64, 128), F32),
            dma((1,)),
            dma((2, 2)),
            dma((2, 1)),
            dma((2, PIECES)),
            dma((2, GROUPS * 2)),
            dma((2, 2 + GROUPS)),
            dma((2, 2 + GROUPS)),
            dma((2, 2 + GROUPS)),
            dma((2, 6)),
        ],
        compiler_params=pltpu.CompilerParams(
            collective_id=0, has_side_effects=True, vmem_limit_bytes=60 * 2**20
        ),
    )(train, target, proj, first, second, owners)


def solution(mesh):
    placed = (
        P("dp", "param"),
        P("dp", "param"),
        P("dp", "param"),
        P("param", "dp", None),
        P("param", "dp", None),
        P("param", None),
    )
    return jax.shard_map(
        per_device, mesh=mesh, in_specs=placed, out_specs=P(("dp", "param"), None), check_vma=False
    )
```

```python
import math

import jax
import jax.numpy as jnp
from jax import lax
from jax.experimental import pallas as pl
from jax.experimental.pallas import tpu as pltpu
from jax.sharding import PartitionSpec as P

MESH = pl.DeviceIdType.MESH
F32, BF16 = jnp.float32, jnp.bfloat16
COLS = 2048
FEATS = 1024
HALF = 512
DEPTH = COLS // 2
SHORT = 512
PIECES = 8
GROUPS = 4
LAST = GROUPS - 1
FAR_FIRST = (2, 6, 5, 7, 1, 3, 4)
XZ_FAR_FIRST = (10, 14, 13, 15, 9, 11, 12, 2, 6, 8, 5, 7, 1, 3, 4)


def one_hot(rows, source_of, along=0):
    r = lax.broadcasted_iota(jnp.int32, (rows, rows), along)
    s = lax.broadcasted_iota(jnp.int32, (rows, rows), 1 - along)
    return jnp.where(source_of(r) == s, 1.0, 0.0).astype(BF16)


def bits(r, low, width):
    return (r >> low) & ((1 << width) - 1)


def kernel(
    train, target, proj, first, second, owner_map,
    out,
    owners, raw_rows, sorted_rows, all_targets, all_proj, columns_of, all_rows, last_long, last_short, all_first, all_second,
    target_lhs, mixed, lhs,
    target_part, target_from_core, target_by_y, target_from_y,
    part, from_core, by_y, from_y, last_part, last_from_core, last_by_y, last_from_y, by_xz, from_xz, raw_unit, unit_cat, own_rows,
    load_sem, mom_sem, target_sem, proj_sem, row_sem, core_sem, y_sem, xz_sem, gather_sem,
    last_core_sem, last_y_sem,
):
    dp = lax.axis_index("dp")
    param = lax.axis_index("param")
    x_hi, y, core = param // 8, (param // 2) % 4, param % 2
    place = x_hi * 8 + dp

    def dp_peer(o):
        return (dp + o) % 8, {"dp": (dp + o) % 8, "param": param}

    core_peer = {"dp": dp, "param": x_hi * 8 + y * 2 + (1 - core)}

    def y_peer(o):
        other = (y + o) % 4
        return other, {"dp": dp, "param": x_hi * 8 + other * 2 + core}

    def xz_peer(o):
        far, near = (x_hi + o // 8) % 2, (dp + o % 8) % 8
        return far * 8 + near, {"dp": near, "param": far * 8 + y * 2 + core}

    def send(src, dst, sems, at, device):
        pltpu.make_async_remote_copy(
            src_ref=src, dst_ref=dst, send_sem=sems.at[0, at], recv_sem=sems.at[1, at],
            device_id=device, device_id_type=MESH,
        ).start()

    def keep(src, dst, sem):
        pltpu.make_async_copy(src, dst, sem).start()

    def wait(ref, sem):
        pltpu.make_async_copy(ref, ref, sem).wait()

    def columns(owner):
        return pl.ds(owner * COLS, COLS)

    barrier = pltpu.get_barrier_semaphore()
    peers = [xz_peer(o)[1] for o in range(1, 16)] + [core_peer] + [y_peer(o)[1] for o in range(1, 4)]
    for device in peers:
        pl.semaphore_signal(barrier, inc=1, device_id=device, device_id_type=MESH)
    keep(train, raw_rows, load_sem.at[0])
    keep(owner_map, owners, load_sem.at[1])
    pl.semaphore_wait(barrier, len(peers))

    def send_targets():
        for o in FAR_FIRST:
            other, device = dp_peer(o)
            send(target.at[:, columns(other)], all_targets.at[dp], target_sem, 0, device)
        keep(target.at[:, columns(dp)], all_targets.at[dp], target_sem.at[1, 0])

    def send_proj(i):
        rows = pl.ds(i * 16, 16)
        for o in FAR_FIRST:
            other, device = dp_peer(o)
            send(proj.at[rows, columns(other)], all_proj.at[i, dp], proj_sem, i, device)
        keep(proj.at[rows, columns(dp)], all_proj.at[i, dp], proj_sem.at[1, i])

    def send_moments():
        for o in FAR_FIRST:
            other, device = dp_peer(o)
            send(first.at[0], all_first.at[dp], mom_sem, 0, device)
            send(second.at[0], all_second.at[dp], mom_sem, 1, device)
        keep(first.at[0], all_first.at[dp], mom_sem.at[1, 0])
        keep(second.at[0], all_second.at[dp], mom_sem.at[1, 1])

    def piece_of(k, half):
        if k < LAST:
            return half * DEPTH, DEPTH, all_rows.at[k * 2 + half]
        return (COLS - SHORT, SHORT, last_short) if half else (0, COLS - SHORT, last_long)

    def send_rows(k, half):
        rows, at = pl.ds(k * 16, 16), k * 2 + half
        start, width, there = piece_of(k, half)

        def some(owner):
            return sorted_rows.at[rows, pl.ds(owner * COLS + start, width)]

        for o in FAR_FIRST:
            other, device = dp_peer(o)
            send(some(other), there.at[dp], row_sem, at, device)
        keep(some(dp), there.at[dp], row_sem.at[1, at])

    def sort_rows():
        wait(raw_rows, load_sem.at[0])
        pick = one_hot(64, lambda r: (r & 15) * 4 + (r >> 4))

        @pl.loop(0, 16)
        def _(t):
            cols = pl.ds(pl.multiple_of(t * 1024, 1024), 1024)
            sorted_rows[:, cols] = jnp.dot(
                pick, raw_rows[:, cols], preferred_element_type=F32
            ).astype(BF16)

    def regroup_targets():
        wait(all_targets, target_sem.at[1, 0])
        regroup = one_hot(
            256,
            lambda r: bits(r, 1, 3) * 32 + bits(r, 4, 1) * 16 + bits(r, 5, 2) * 4
            + bits(r, 7, 1) * 2 + bits(r, 0, 1),
        )

        @pl.loop(0, 8)
        def _(t):
            cols = pl.ds(pl.multiple_of(t * 256, 256), 256)
            target_lhs[:, cols] = jnp.dot(
                regroup, all_targets[:, :, cols].reshape(256, 256), preferred_element_type=F32
            ).astype(BF16)

    def transpose(i):
        wait(all_proj.at[i], proj_sem.at[1, i])
        same = one_hot(256, lambda r: r)
        for t in range(8):
            at = slice(t * 256, (t + 1) * 256)
            columns_of[at, i * 128 : (i + 1) * 128] = lax.dot_general(
                same, all_proj[i, :, :, at].reshape(128, 256), (((1,), (1,)), ((), ())),
                preferred_element_type=F32,
            ).astype(BF16)

    def multiply_targets(h):
        target_part[h] = jnp.dot(
            target_lhs[...], columns_of[:, h * HALF : (h + 1) * HALF], preferred_element_type=F32
        )
        away = pl.ds((1 - core) * 128, 128)
        send(target_part.at[h, away], target_from_core.at[h], core_sem, h, core_peer)

    def multiply(k, half):
        at = k * 2 + half
        start, width, here = piece_of(k, half)
        wait(here, row_sem.at[1, at])

        @pl.loop(0, 8)
        def _(s):
            for t in range(width // 512):
                cols = slice(t * 512, (t + 1) * 512)
                own = slice(start + t * 512, start + (t + 1) * 512)
                g = here[s, :, cols].astype(F32)
                upper = first_row[:, own] + 0.1 * g
                lower = jnp.sqrt(second_row[:, own] + 0.001 * g * g) + 1e-08
                mixed[s, :, cols] = (upper / lower).astype(BF16)

        for t in range(width // 512):
            cols = slice(t * 512, (t + 1) * 512)
            lhs[:, cols] = jnp.dot(
                regroup, mixed[:, :, cols].reshape(128, 512), preferred_element_type=F32
            ).astype(BF16)
        away = pl.ds((1 - core) * 64, 64)
        for h in range(2):
            cols = slice(h * HALF, (h + 1) * HALF)
            done = jnp.dot(
                lhs[:, 0:width], columns_of[start : start + width, cols],
                preferred_element_type=F32,
            )
            part[k, :, cols] = done if half == 0 else part[k, :, cols] + done
            if half == 1 and k == LAST:
                last_part[h] = part[k, away, cols].astype(BF16)
                send(last_part.at[h], last_from_core.at[h], last_core_sem, h, core_peer)
        if half == 1 and k < LAST:
            send(part.at[k, away], from_core.at[k], core_sem, 2 + k, core_peer)

    def add_core(g):
        if g < 2:
            here, there, total, arrived, k, rows = (
                target_part, target_from_core, target_by_y, target_from_y, g, 32,
            )
        else:
            here, there, total, arrived, k, rows = part, from_core, by_y, from_y, g - 2, 16
        wait(there.at[k], core_sem.at[1, g])

        @pl.loop(0, 4)
        def _(t):
            at = pl.ds(t * rows, rows)
            total[k, at] = here[k, pl.ds((core * 4 + t) * rows, rows)] + there[k, at]

        for o in (2, 1, 3):
            other, device = y_peer(o)
            send(total.at[k, pl.ds(other * rows, rows)], arrived.at[k, o - 1], y_sem, g, device)

    def add_core_last(h):
        cols = slice(h * HALF, (h + 1) * HALF)
        wait(last_from_core.at[h], last_core_sem.at[1, h])
        total = part[LAST, pl.ds(core * 64, 64), cols] + last_from_core[h].astype(F32)
        by_y[LAST, :, cols] = total
        last_by_y[h] = total.astype(BF16)
        for o in (2, 1, 3):
            other, device = y_peer(o)
            rows = pl.ds(other * 16, 16)
            send(last_by_y.at[h, rows], last_from_y.at[h, o - 1], last_y_sem, h, device)

    def add_y(g):
        if g == 5:
            total, k, rows = by_y, LAST, 16
            for h in range(2):
                wait(last_from_y.at[h], last_y_sem.at[1, h])
        elif g < 2:
            total, arrived, k, rows = target_by_y, target_from_y, g, 32
        else:
            total, arrived, k, rows = by_y, from_y, g - 2, 16
        done = total[k, pl.ds(y * rows, rows)]
        if g < 5:
            wait(arrived.at[k], y_sem.at[1, g])
            done = done + arrived[k, 0] + arrived[k, 1] + arrived[k, 2]
        else:
            for o in range(3):
                both = [last_from_y[h, o].astype(F32) for h in range(2)]
                done = done + jnp.concatenate(both, axis=1)
        tiles = 128 // rows
        for s in range(tiles):
            by_xz[g, pl.ds(s, rows, stride=tiles), :] = done[:, s * 128 : (s + 1) * 128]
        for o in XZ_FAR_FIRST:
            other, device = xz_peer(o)
            send(by_xz.at[g, pl.ds(other * 8, 8)], from_xz.at[g, pl.ds(o * 8 - 8, 8)], xz_sem, g, device)

    def add_xz(g):
        wait(from_xz.at[g], xz_sem.at[1, g])
        f = by_xz[g, pl.ds(place * 8, 8)]
        for o in range(15):
            f = f + from_xz[g, o * 8 : o * 8 + 8]
        return f

    spot = (core * 4 + y) * 16 + place

    def gather_xz(h):
        mine = raw_unit.at[h, pl.ds(spot * 8, 8)]
        raw_unit[h, pl.ds(spot * 8, 8)] = add_xz(h)
        for o in XZ_FAR_FIRST:
            send(mine, mine, gather_sem, h * 3, xz_peer(o)[1])

    def gather_y(h):
        wait(raw_unit.at[h, pl.ds(0, 120)], gather_sem.at[1, h * 3])
        mine = raw_unit.at[h, pl.ds((core * 4 + y) * 128, 128)]
        for o in (2, 1, 3):
            send(mine, mine, gather_sem, h * 3 + 1, y_peer(o)[1])

    def gather_core(h):
        wait(raw_unit.at[h, pl.ds(0, 384)], gather_sem.at[1, h * 3 + 1])
        mine = raw_unit.at[h, pl.ds(core * 512, 512)]
        send(mine, mine, gather_sem, h * 3 + 2, core_peer)

    def arrange():
        for h in range(2):
            wait(raw_unit.at[h, pl.ds(0, 512)], gather_sem.at[1, h * 3 + 2])
        natural = one_hot(
            256,
            lambda r: bits(r, 0, 1) * 128 + bits(r, 1, 1) * 64 + bits(r, 2, 2) * 16
            + bits(r, 4, 1) * 8 + bits(r, 5, 3),
            along=1,
        )

        def piece(h, s, c):
            return raw_unit[h, pl.ds(c * 4 + s, 128, stride=8), :]

        scale = []
        for c in range(2):
            squares = jnp.zeros((128, 128), F32)
            for h in range(2):
                for s in range(4):
                    f = piece(h, s, c)
                    squares = squares + f * f
            mean = jnp.sum(squares, axis=1, keepdims=True) / FEATS
            scale.append(lax.rsqrt(mean + 1e-06))
        for h in range(2):
            for s in range(4):
                f = jnp.concatenate([(piece(h, s, c) * scale[c]).T for c in range(2)], axis=1)
                high = f.astype(BF16)
                low = (f - high.astype(F32)).astype(BF16)
                at = slice(h * HALF + s * 128, h * HALF + (s + 1) * 128)
                unit_cat[at, 0:256] = jnp.dot(high, natural, preferred_element_type=F32).astype(BF16)
                unit_cat[at, 256:512] = jnp.dot(low, natural, preferred_element_type=F32).astype(BF16)

    def train_row(g):
        f = add_xz(g)
        mean = jnp.sum(f * f, keepdims=True) / FEATS
        own_rows[(g - 2) * 8 : (g - 1) * 8] = f * lax.rsqrt(mean + 1e-06)

    def sent():
        wait(all_targets.at[pl.ds(0, 7)], target_sem.at[0, 0])
        wait(all_first.at[pl.ds(0, 7)], mom_sem.at[0, 0])
        wait(all_second.at[pl.ds(0, 7)], mom_sem.at[0, 1])
        for i in range(PIECES):
            wait(all_proj.at[i, pl.ds(0, 7)], proj_sem.at[0, i])
        for h in range(2):
            wait(target_from_core.at[h], core_sem.at[0, h])
            wait(target_from_y.at[h], y_sem.at[0, h])
            wait(from_xz.at[h], xz_sem.at[0, h])
            wait(raw_unit.at[h, pl.ds(0, 120)], gather_sem.at[0, h * 3])
            wait(raw_unit.at[h, pl.ds(0, 384)], gather_sem.at[0, h * 3 + 1])
            wait(raw_unit.at[h, pl.ds(0, 512)], gather_sem.at[0, h * 3 + 2])
        for h in range(2):
            wait(piece_of(LAST, h)[2].at[pl.ds(0, 7)], row_sem.at[0, LAST * 2 + h])
            wait(last_from_core.at[h], last_core_sem.at[0, h])
            wait(last_from_y.at[h], last_y_sem.at[0, h])
        for k in range(LAST):
            for h in range(2):
                wait(all_rows.at[k * 2 + h, pl.ds(0, 7)], row_sem.at[0, k * 2 + h])
            wait(from_core.at[k], core_sem.at[0, 2 + k])
            wait(from_y.at[k], y_sem.at[0, 2 + k])
            wait(from_xz.at[2 + k], xz_sem.at[0, 2 + k])

    send_targets()
    send_proj(0)
    send_moments()
    send_proj(1)
    own_rows[...] = jnp.zeros_like(own_rows)
    sort_rows()
    regroup_targets()
    send_proj(2)
    transpose(0)
    send_proj(3)
    transpose(1)
    send_proj(4)
    wait(all_first, mom_sem.at[1, 0])
    wait(all_second, mom_sem.at[1, 1])
    pltpu.make_async_copy(owner_map, owners, load_sem.at[1]).wait()
    owner = owners[0, dp]
    first_row = 0.9 * all_first[owner]
    second_row = 0.999 * all_second[owner]
    regroup = one_hot(
        128, lambda r: bits(r, 0, 3) * 16 + bits(r, 3, 1) * 8 + bits(r, 4, 2) * 2 + bits(r, 6, 1)
    )

    transpose(2)
    send_proj(5)
    transpose(3)
    multiply_targets(0)
    send_proj(6)
    add_core(0)
    transpose(4)
    send_proj(7)
    transpose(5)
    add_y(0)
    send_rows(0, 0)
    send_rows(0, 1)
    transpose(6)
    send_rows(1, 0)
    transpose(7)
    multiply_targets(1)
    gather_xz(0)
    send_rows(1, 1)
    add_core(1)
    multiply(0, 0)
    multiply(0, 1)
    add_y(1)
    send_rows(2, 0)
    gather_y(0)
    send_rows(2, 1)
    add_core(2)
    multiply(1, 0)
    multiply(1, 1)
    gather_xz(1)
    send_rows(3, 0)
    send_rows(3, 1)
    add_core(3)
    add_y(2)
    gather_core(0)
    multiply(2, 0)
    multiply(2, 1)
    gather_y(1)
    add_y(3)
    add_core(4)
    multiply(3, 0)
    multiply(3, 1)
    add_core_last(0)
    add_core_last(1)
    gather_core(1)
    add_y(4)
    train_row(2)
    train_row(3)
    arrange()
    add_y(5)
    sent()
    train_row(4)
    train_row(5)

    rows = jnp.concatenate([own_rows[pl.ds(s, 8, stride=8), :] for s in range(8)], axis=1)
    high = rows.astype(BF16)
    low = (rows - high.astype(F32)).astype(BF16)
    product = jnp.dot(
        jnp.concatenate([high, low], axis=0), unit_cat[...], preferred_element_type=F32
    )
    scaled = product[0:8, 0:256] + (product[8:16, 0:256] + product[0:8, 256:512])
    out[...] = scaled[0:4] / math.sqrt(FEATS)

    wait(from_xz.at[5], xz_sem.at[0, 5])


def per_device(train, target, proj, first, second, owners):
    vmem = pltpu.VMEM
    dma = pltpu.SemaphoreType.DMA
    anywhere = pl.BlockSpec(memory_space=pl.ANY)
    return pl.pallas_call(
        kernel,
        out_shape=jax.ShapeDtypeStruct((4, 256), F32),
        in_specs=[anywhere] * 6,
        out_specs=pl.BlockSpec(memory_space=pltpu.VMEM),
        scratch_shapes=[
            pltpu.SMEM((1, 8), jnp.int32),
            vmem((64, 16384), BF16),
            vmem((64, 16384), BF16),
            vmem((8, 32, COLS), BF16),
            vmem((PIECES, 8, 16, COLS), BF16),
            vmem((COLS, FEATS), BF16),
            vmem((LAST * 2, 8, 16, DEPTH), BF16),
            vmem((8, 16, COLS - SHORT), BF16),
            vmem((8, 16, SHORT), BF16),
            vmem((8, 1, COLS), F32),
            vmem((8, 1, COLS), F32),
            vmem((256, COLS), BF16),
            vmem((8, 16, COLS - SHORT), BF16),
            vmem((128, COLS - SHORT), BF16),
            vmem((2, 256, HALF), F32),
            vmem((2, 128, HALF), F32),
            vmem((2, 128, HALF), F32),
            vmem((2, 3, 32, HALF), F32),
            vmem((GROUPS, 128, FEATS), F32),
            vmem((LAST, 64, FEATS), F32),
            vmem((GROUPS, 64, FEATS), F32),
            vmem((LAST, 3, 16, FEATS), F32),
            vmem((2, 64, HALF), BF16),
            vmem((2, 64, HALF), BF16),
            vmem((2, 64, HALF), BF16),
            vmem((2, 3, 16, HALF), BF16),
            vmem((2 + GROUPS, 128, 128), F32),
            vmem((2 + GROUPS, 120, 128), F32),
            vmem((2, 1024, 128), F32),
            vmem((FEATS, 512), BF16),
            vmem((64, 128), F32),
            dma((2,)),
            dma((2, 2)),
            dma((2, 1)),
            dma((2, PIECES)),
            dma((2, GROUPS * 2)),
            dma((2, 2 + LAST)),
            dma((2, 2 + LAST)),
            dma((2, 2 + GROUPS)),
            dma((2, 6)),
            dma((2, 2)),
            dma((2, 2)),
        ],
        compiler_params=pltpu.CompilerParams(
            collective_id=0, has_side_effects=True, vmem_limit_bytes=60 * 2**20
        ),
    )(train, target, proj, first, second, owners)


def solution(mesh):
    placed = (
        P("dp", "param"),
        P("dp", "param"),
        P("dp", "param"),
        P("param", "dp", None),
        P("param", "dp", None),
        P("param", None),
    )
    return jax.shard_map(
        per_device, mesh=mesh, in_specs=placed, out_specs=P(("dp", "param"), None), check_vma=False
    )
```

```python
import math

import jax
import jax.numpy as jnp
from jax import lax
from jax.experimental import pallas as pl
from jax.experimental.pallas import tpu as pltpu
from jax.sharding import PartitionSpec as P

MESH = pl.DeviceIdType.MESH
F32, BF16 = jnp.float32, jnp.bfloat16
COLS = 2048
FEATS = 1024
HALF = 512
DEPTH = COLS // 2
SHORT = 512
PIECES = 8
GROUPS = 4
LAST = GROUPS - 1
FAR_FIRST = (2, 6, 5, 7, 1, 3, 4)
XZ_FAR_FIRST = (10, 14, 13, 15, 9, 11, 12, 2, 6, 8, 5, 7, 1, 3, 4)


def one_hot(rows, source_of, along=0):
    r = lax.broadcasted_iota(jnp.int32, (rows, rows), along)
    s = lax.broadcasted_iota(jnp.int32, (rows, rows), 1 - along)
    return jnp.where(source_of(r) == s, 1.0, 0.0).astype(BF16)


def bits(r, low, width):
    return (r >> low) & ((1 << width) - 1)


def kernel(
    train, target, proj, first, second, owner_map,
    out,
    owners, raw_rows, sorted_rows, all_targets, all_proj, columns_of, all_rows, last_long, last_short, all_first, all_second,
    target_lhs, mixed, lhs,
    target_part, target_from_core, target_by_y, target_from_y,
    part, from_core, by_y, from_y, last_part, last_from_core, last_by_y, last_from_y, by_xz, from_xz, raw_unit, unit_cat, own_rows,
    load_sem, mom_sem, target_sem, proj_sem, row_sem, core_sem, y_sem, xz_sem, gather_sem,
    last_core_sem, last_y_sem,
):
    dp = lax.axis_index("dp")
    param = lax.axis_index("param")
    x_hi, y, core = param // 8, (param // 2) % 4, param % 2
    place = x_hi * 8 + dp

    def dp_peer(o):
        return (dp + o) % 8, {"dp": (dp + o) % 8, "param": param}

    core_peer = {"dp": dp, "param": x_hi * 8 + y * 2 + (1 - core)}

    def y_peer(o):
        other = (y + o) % 4
        return other, {"dp": dp, "param": x_hi * 8 + other * 2 + core}

    def xz_peer(o):
        far, near = (x_hi + o // 8) % 2, (dp + o % 8) % 8
        return far * 8 + near, {"dp": near, "param": far * 8 + y * 2 + core}

    def send(src, dst, sems, at, device):
        pltpu.make_async_remote_copy(
            src_ref=src, dst_ref=dst, send_sem=sems.at[0, at], recv_sem=sems.at[1, at],
            device_id=device, device_id_type=MESH,
        ).start()

    def keep(src, dst, sem):
        pltpu.make_async_copy(src, dst, sem).start()

    def wait(ref, sem):
        pltpu.make_async_copy(ref, ref, sem).wait()

    def columns(owner):
        return pl.ds(owner * COLS, COLS)

    barrier = pltpu.get_barrier_semaphore()
    peers = [xz_peer(o)[1] for o in range(1, 16)] + [core_peer] + [y_peer(o)[1] for o in range(1, 4)]
    for device in peers:
        pl.semaphore_signal(barrier, inc=1, device_id=device, device_id_type=MESH)
    keep(train, raw_rows, load_sem.at[0])
    keep(owner_map, owners, load_sem.at[1])
    pl.semaphore_wait(barrier, len(peers))

    def send_targets():
        for o in FAR_FIRST:
            other, device = dp_peer(o)
            send(target.at[:, columns(other)], all_targets.at[dp], target_sem, 0, device)
        keep(target.at[:, columns(dp)], all_targets.at[dp], target_sem.at[1, 0])

    def send_proj(i):
        rows = pl.ds(i * 16, 16)
        for o in FAR_FIRST:
            other, device = dp_peer(o)
            send(proj.at[rows, columns(other)], all_proj.at[i, dp], proj_sem, i, device)
        keep(proj.at[rows, columns(dp)], all_proj.at[i, dp], proj_sem.at[1, i])

    def send_moments():
        for o in FAR_FIRST:
            other, device = dp_peer(o)
            send(first.at[0], all_first.at[dp], mom_sem, 0, device)
            send(second.at[0], all_second.at[dp], mom_sem, 1, device)
        keep(first.at[0], all_first.at[dp], mom_sem.at[1, 0])
        keep(second.at[0], all_second.at[dp], mom_sem.at[1, 1])

    def piece_of(k, half):
        if k < LAST:
            return half * DEPTH, DEPTH, all_rows.at[k * 2 + half]
        return (COLS - SHORT, SHORT, last_short) if half else (0, COLS - SHORT, last_long)

    def send_rows(k, half):
        rows, at = pl.ds(k * 16, 16), k * 2 + half
        start, width, there = piece_of(k, half)

        def some(owner):
            return sorted_rows.at[rows, pl.ds(owner * COLS + start, width)]

        for o in FAR_FIRST:
            other, device = dp_peer(o)
            send(some(other), there.at[dp], row_sem, at, device)
        keep(some(dp), there.at[dp], row_sem.at[1, at])

    def sort_rows():
        wait(raw_rows, load_sem.at[0])
        pick = one_hot(64, lambda r: (r & 15) * 4 + (r >> 4))

        @pl.loop(0, 16)
        def _(t):
            cols = pl.ds(pl.multiple_of(t * 1024, 1024), 1024)
            sorted_rows[:, cols] = jnp.dot(
                pick, raw_rows[:, cols], preferred_element_type=F32
            ).astype(BF16)

    def regroup_targets():
        wait(all_targets, target_sem.at[1, 0])
        regroup = one_hot(
            256,
            lambda r: bits(r, 1, 3) * 32 + bits(r, 4, 1) * 16 + bits(r, 5, 2) * 4
            + bits(r, 7, 1) * 2 + bits(r, 0, 1),
        )

        @pl.loop(0, 8)
        def _(t):
            cols = pl.ds(pl.multiple_of(t * 256, 256), 256)
            target_lhs[:, cols] = jnp.dot(
                regroup, all_targets[:, :, cols].reshape(256, 256), preferred_element_type=F32
            ).astype(BF16)

    def transpose(i):
        wait(all_proj.at[i], proj_sem.at[1, i])
        same = one_hot(256, lambda r: r)
        for t in range(8):
            at = slice(t * 256, (t + 1) * 256)
            columns_of[at, i * 128 : (i + 1) * 128] = lax.dot_general(
                same, all_proj[i, :, :, at].reshape(128, 256), (((1,), (1,)), ((), ())),
                preferred_element_type=F32,
            ).astype(BF16)

    def multiply_targets(h):
        target_part[h] = jnp.dot(
            target_lhs[...], columns_of[:, h * HALF : (h + 1) * HALF], preferred_element_type=F32
        )
        away = pl.ds((1 - core) * 128, 128)
        send(target_part.at[h, away], target_from_core.at[h], core_sem, h, core_peer)

    def multiply(k, half):
        at = k * 2 + half
        start, width, here = piece_of(k, half)
        wait(here, row_sem.at[1, at])

        @pl.loop(0, 8)
        def _(s):
            for t in range(width // 512):
                cols = slice(t * 512, (t + 1) * 512)
                own = slice(start + t * 512, start + (t + 1) * 512)
                g = here[s, :, cols].astype(F32)
                upper = first_row[:, own] + 0.1 * g
                lower = jnp.sqrt(second_row[:, own] + 0.001 * g * g) + 1e-08
                mixed[s, :, cols] = (upper / lower).astype(BF16)

        for t in range(width // 512):
            cols = slice(t * 512, (t + 1) * 512)
            lhs[:, cols] = jnp.dot(
                regroup, mixed[:, :, cols].reshape(128, 512), preferred_element_type=F32
            ).astype(BF16)
        away = pl.ds((1 - core) * 64, 64)
        for h in range(2):
            cols = slice(h * HALF, (h + 1) * HALF)
            done = jnp.dot(
                lhs[:, 0:width], columns_of[start : start + width, cols],
                preferred_element_type=F32,
            )
            part[k, :, cols] = done if half == 0 else part[k, :, cols] + done
            if half == 1 and k == LAST:
                last_part[h] = part[k, away, cols].astype(BF16)
                send(last_part.at[h], last_from_core.at[h], last_core_sem, h, core_peer)
        if half == 1 and k < LAST:
            send(part.at[k, away], from_core.at[k], core_sem, 2 + k, core_peer)

    def add_core(g):
        if g < 2:
            here, there, total, arrived, k, rows = (
                target_part, target_from_core, target_by_y, target_from_y, g, 32,
            )
        else:
            here, there, total, arrived, k, rows = part, from_core, by_y, from_y, g - 2, 16
        wait(there.at[k], core_sem.at[1, g])

        @pl.loop(0, 4)
        def _(t):
            at = pl.ds(t * rows, rows)
            total[k, at] = here[k, pl.ds((core * 4 + t) * rows, rows)] + there[k, at]

        for o in (2, 1, 3):
            other, device = y_peer(o)
            send(total.at[k, pl.ds(other * rows, rows)], arrived.at[k, o - 1], y_sem, g, device)

    def add_core_last(h):
        cols = slice(h * HALF, (h + 1) * HALF)
        wait(last_from_core.at[h], last_core_sem.at[1, h])
        total = part[LAST, pl.ds(core * 64, 64), cols] + last_from_core[h].astype(F32)
        by_y[LAST, :, cols] = total
        last_by_y[h] = total.astype(BF16)
        for o in (2, 1, 3):
            other, device = y_peer(o)
            rows = pl.ds(other * 16, 16)
            send(last_by_y.at[h, rows], last_from_y.at[h, o - 1], last_y_sem, h, device)

    def add_y(g):
        if g == 5:
            total, k, rows = by_y, LAST, 16
            for h in range(2):
                wait(last_from_y.at[h], last_y_sem.at[1, h])
        elif g < 2:
            total, arrived, k, rows = target_by_y, target_from_y, g, 32
        else:
            total, arrived, k, rows = by_y, from_y, g - 2, 16
        done = total[k, pl.ds(y * rows, rows)]
        if g < 5:
            wait(arrived.at[k], y_sem.at[1, g])
            done = done + arrived[k, 0] + arrived[k, 1] + arrived[k, 2]
        else:
            for o in range(3):
                both = [last_from_y[h, o].astype(F32) for h in range(2)]
                done = done + jnp.concatenate(both, axis=1)
        tiles = 128 // rows
        for s in range(tiles):
            by_xz[g, pl.ds(s, rows, stride=tiles), :] = done[:, s * 128 : (s + 1) * 128]
        for o in XZ_FAR_FIRST:
            other, device = xz_peer(o)
            send(by_xz.at[g, pl.ds(other * 8, 8)], from_xz.at[g, pl.ds(o * 8 - 8, 8)], xz_sem, g, device)

    def add_xz(g):
        wait(from_xz.at[g], xz_sem.at[1, g])
        f = by_xz[g, pl.ds(place * 8, 8)]
        for o in range(15):
            f = f + from_xz[g, o * 8 : o * 8 + 8]
        return f

    spot = (core * 4 + y) * 16 + place

    def gather_xz(h):
        mine = raw_unit.at[h, pl.ds(spot * 8, 8)]
        raw_unit[h, pl.ds(spot * 8, 8)] = add_xz(h)
        for o in XZ_FAR_FIRST:
            send(mine, mine, gather_sem, h * 3, xz_peer(o)[1])

    def gather_y(h):
        wait(raw_unit.at[h, pl.ds(0, 120)], gather_sem.at[1, h * 3])
        mine = raw_unit.at[h, pl.ds((core * 4 + y) * 128, 128)]
        for o in (2, 1, 3):
            send(mine, mine, gather_sem, h * 3 + 1, y_peer(o)[1])

    def gather_core(h):
        wait(raw_unit.at[h, pl.ds(0, 384)], gather_sem.at[1, h * 3 + 1])
        mine = raw_unit.at[h, pl.ds(core * 512, 512)]
        send(mine, mine, gather_sem, h * 3 + 2, core_peer)

    def arrange():
        for h in range(2):
            wait(raw_unit.at[h, pl.ds(0, 512)], gather_sem.at[1, h * 3 + 2])
        natural = one_hot(
            256,
            lambda r: bits(r, 0, 1) * 128 + bits(r, 1, 1) * 64 + bits(r, 2, 2) * 16
            + bits(r, 4, 1) * 8 + bits(r, 5, 3),
            along=1,
        )

        def piece(h, s, c):
            return raw_unit[h, pl.ds(c * 4 + s, 128, stride=8), :]

        scale = []
        for c in range(2):
            squares = jnp.zeros((128, 128), F32)
            for h in range(2):
                for s in range(4):
                    f = piece(h, s, c)
                    squares = squares + f * f
            mean = jnp.sum(squares, axis=1, keepdims=True) / FEATS
            scale.append(lax.rsqrt(mean + 1e-06))
        for h in range(2):
            for s in range(4):
                f = jnp.concatenate([(piece(h, s, c) * scale[c]).T for c in range(2)], axis=1)
                high = f.astype(BF16)
                low = (f - high.astype(F32)).astype(BF16)
                at = slice(h * HALF + s * 128, h * HALF + (s + 1) * 128)
                unit_cat[at, 0:256] = jnp.dot(high, natural, preferred_element_type=F32).astype(BF16)
                unit_cat[at, 256:512] = jnp.dot(low, natural, preferred_element_type=F32).astype(BF16)

    def train_row(g):
        f = add_xz(g)
        mean = jnp.sum(f * f, keepdims=True) / FEATS
        own_rows[(g - 2) * 8 : (g - 1) * 8] = f * lax.rsqrt(mean + 1e-06)

    def sent():
        wait(all_targets.at[pl.ds(0, 7)], target_sem.at[0, 0])
        wait(all_first.at[pl.ds(0, 7)], mom_sem.at[0, 0])
        wait(all_second.at[pl.ds(0, 7)], mom_sem.at[0, 1])
        for i in range(PIECES):
            wait(all_proj.at[i, pl.ds(0, 7)], proj_sem.at[0, i])
        for h in range(2):
            wait(target_from_core.at[h], core_sem.at[0, h])
            wait(target_from_y.at[h], y_sem.at[0, h])
            wait(from_xz.at[h], xz_sem.at[0, h])
            wait(raw_unit.at[h, pl.ds(0, 120)], gather_sem.at[0, h * 3])
            wait(raw_unit.at[h, pl.ds(0, 384)], gather_sem.at[0, h * 3 + 1])
            wait(raw_unit.at[h, pl.ds(0, 512)], gather_sem.at[0, h * 3 + 2])
        for h in range(2):
            wait(piece_of(LAST, h)[2].at[pl.ds(0, 7)], row_sem.at[0, LAST * 2 + h])
            wait(last_from_core.at[h], last_core_sem.at[0, h])
            wait(last_from_y.at[h], last_y_sem.at[0, h])
        for k in range(LAST):
            for h in range(2):
                wait(all_rows.at[k * 2 + h, pl.ds(0, 7)], row_sem.at[0, k * 2 + h])
            wait(from_core.at[k], core_sem.at[0, 2 + k])
            wait(from_y.at[k], y_sem.at[0, 2 + k])
            wait(from_xz.at[2 + k], xz_sem.at[0, 2 + k])

    send_targets()
    send_proj(0)
    send_moments()
    send_proj(1)
    own_rows[...] = jnp.zeros_like(own_rows)
    sort_rows()
    regroup_targets()
    send_proj(2)
    transpose(0)
    send_proj(3)
    transpose(1)
    send_proj(4)
    wait(all_first, mom_sem.at[1, 0])
    wait(all_second, mom_sem.at[1, 1])
    pltpu.make_async_copy(owner_map, owners, load_sem.at[1]).wait()
    owner = owners[0, dp]
    first_row = 0.9 * all_first[owner]
    second_row = 0.999 * all_second[owner]
    regroup = one_hot(
        128, lambda r: bits(r, 0, 3) * 16 + bits(r, 3, 1) * 8 + bits(r, 4, 2) * 2 + bits(r, 6, 1)
    )

    transpose(2)
    send_proj(5)
    transpose(3)
    multiply_targets(0)
    send_proj(6)
    add_core(0)
    transpose(4)
    send_proj(7)
    transpose(5)
    add_y(0)
    send_rows(0, 0)
    send_rows(0, 1)
    transpose(6)
    send_rows(1, 0)
    transpose(7)
    multiply_targets(1)
    gather_xz(0)
    send_rows(1, 1)
    add_core(1)
    multiply(0, 0)
    multiply(0, 1)
    add_y(1)
    send_rows(2, 0)
    gather_y(0)
    send_rows(2, 1)
    add_core(2)
    multiply(1, 0)
    multiply(1, 1)
    gather_xz(1)
    send_rows(3, 0)
    send_rows(3, 1)
    add_core(3)
    add_y(2)
    gather_core(0)
    multiply(2, 0)
    multiply(2, 1)
    gather_y(1)
    add_y(3)
    add_core(4)
    multiply(3, 0)
    multiply(3, 1)
    add_core_last(0)
    add_core_last(1)
    gather_core(1)
    add_y(4)
    train_row(2)
    train_row(3)
    arrange()
    add_y(5)
    sent()
    train_row(4)
    train_row(5)

    rows = jnp.concatenate([own_rows[pl.ds(s, 8, stride=8), :] for s in range(8)], axis=1)
    high = rows.astype(BF16)
    low = (rows - high.astype(F32)).astype(BF16)
    product = jnp.dot(
        jnp.concatenate([high, low], axis=0), unit_cat[...], preferred_element_type=F32
    )
    scaled = product[0:8, 0:256] + (product[8:16, 0:256] + product[0:8, 256:512])
    out[...] = scaled[0:4] / math.sqrt(FEATS)

    wait(from_xz.at[5], xz_sem.at[0, 5])


def per_device(train, target, proj, first, second, owners):
    vmem = pltpu.VMEM
    dma = pltpu.SemaphoreType.DMA
    anywhere = pl.BlockSpec(memory_space=pl.ANY)
    return pl.pallas_call(
        kernel,
        out_shape=jax.ShapeDtypeStruct((4, 256), F32),
        in_specs=[anywhere] * 6,
        out_specs=pl.BlockSpec(memory_space=pltpu.VMEM),
        scratch_shapes=[
            pltpu.SMEM((1, 8), jnp.int32),
            vmem((64, 16384), BF16),
            vmem((64, 16384), BF16),
            vmem((8, 32, COLS), BF16),
            vmem((PIECES, 8, 16, COLS), BF16),
            vmem((COLS, FEATS), BF16),
            vmem((LAST * 2, 8, 16, DEPTH), BF16),
            vmem((8, 16, COLS - SHORT), BF16),
            vmem((8, 16, SHORT), BF16),
            vmem((8, 1, COLS), F32),
            vmem((8, 1, COLS), F32),
            vmem((256, COLS), BF16),
            vmem((8, 16, COLS - SHORT), BF16),
            vmem((128, COLS - SHORT), BF16),
            vmem((2, 256, HALF), F32),
            vmem((2, 128, HALF), F32),
            vmem((2, 128, HALF), F32),
            vmem((2, 3, 32, HALF), F32),
            vmem((GROUPS, 128, FEATS), F32),
            vmem((LAST, 64, FEATS), F32),
            vmem((GROUPS, 64, FEATS), F32),
            vmem((LAST, 3, 16, FEATS), F32),
            vmem((2, 64, HALF), BF16),
            vmem((2, 64, HALF), BF16),
            vmem((2, 64, HALF), BF16),
            vmem((2, 3, 16, HALF), BF16),
            vmem((2 + GROUPS, 128, 128), F32),
            vmem((2 + GROUPS, 120, 128), F32),
            vmem((2, 1024, 128), F32),
            vmem((FEATS, 512), BF16),
            vmem((64, 128), F32),
            dma((2,)),
            dma((2, 2)),
            dma((2, 1)),
            dma((2, PIECES)),
            dma((2, GROUPS * 2)),
            dma((2, 2 + LAST)),
            dma((2, 2 + LAST)),
            dma((2, 2 + GROUPS)),
            dma((2, 6)),
            dma((2, 2)),
            dma((2, 2)),
        ],
        compiler_params=pltpu.CompilerParams(
            collective_id=0, has_side_effects=True, vmem_limit_bytes=40 * 2**20
        ),
    )(*(pltpu.with_memory_space_constraint(a, pltpu.HBM) for a in (train, target, proj, first, second, owners)))


def solution(mesh):
    placed = (
        P("dp", "param"),
        P("dp", "param"),
        P("dp", "param"),
        P("param", "dp", None),
        P("param", "dp", None),
        P("param", None),
    )
    return jax.shard_map(
        per_device, mesh=mesh, in_specs=placed, out_specs=P(("dp", "param"), None), check_vma=False
    )
```

```python
import math

import jax
import jax.numpy as jnp
from jax import lax
from jax.experimental import pallas as pl
from jax.experimental.pallas import tpu as pltpu
from jax.sharding import PartitionSpec as P

MESH = pl.DeviceIdType.MESH
F32, BF16 = jnp.float32, jnp.bfloat16
COLS = 2048
FEATS = 1024
HALF = 512
DEPTH = COLS // 2
SHORT = 512
PIECES = 8
GROUPS = 4
LAST = GROUPS - 1
FAR_FIRST = (2, 6, 5, 7, 1, 3, 4)
XZ_FAR_FIRST = (10, 14, 13, 15, 9, 11, 12, 2, 6, 8, 5, 7, 1, 3, 4)


def one_hot(rows, source_of, along=0):
    r = lax.broadcasted_iota(jnp.int32, (rows, rows), along)
    s = lax.broadcasted_iota(jnp.int32, (rows, rows), 1 - along)
    return jnp.where(source_of(r) == s, 1.0, 0.0).astype(BF16)


def bits(r, low, width):
    return (r >> low) & ((1 << width) - 1)


def kernel(
    train, target, proj, first, second, owner_map,
    out,
    owners, raw_rows, sorted_rows, all_targets, all_proj, columns_of, all_rows, last_long, last_short, all_first, all_second,
    target_lhs, mixed, lhs,
    target_part, target_from_core, target_by_y, target_from_y,
    part, from_core, by_y, from_y, last_part, last_from_core, last_by_y, last_from_y, by_xz, from_xz, raw_unit, unit_cat, own_rows,
    load_sem, mom_sem, target_sem, proj_sem, row_sem, core_sem, y_sem, xz_sem, gather_sem,
    last_core_sem, last_y_sem,
):
    dp = lax.axis_index("dp")
    param = lax.axis_index("param")
    x_hi, y, core = param // 8, (param // 2) % 4, param % 2
    place = x_hi * 8 + dp

    def dp_peer(o):
        return (dp + o) % 8, {"dp": (dp + o) % 8, "param": param}

    core_peer = {"dp": dp, "param": x_hi * 8 + y * 2 + (1 - core)}

    def y_peer(o):
        other = (y + o) % 4
        return other, {"dp": dp, "param": x_hi * 8 + other * 2 + core}

    def xz_peer(o):
        far, near = (x_hi + o // 8) % 2, (dp + o % 8) % 8
        return far * 8 + near, {"dp": near, "param": far * 8 + y * 2 + core}

    def send(src, dst, sems, at, device):
        pltpu.make_async_remote_copy(
            src_ref=src, dst_ref=dst, send_sem=sems.at[0, at], recv_sem=sems.at[1, at],
            device_id=device, device_id_type=MESH,
        ).start()

    def keep(src, dst, sem):
        pltpu.make_async_copy(src, dst, sem).start()

    def wait(ref, sem):
        pltpu.make_async_copy(ref, ref, sem).wait()

    def columns(owner):
        return pl.ds(owner * COLS, COLS)

    barrier = pltpu.get_barrier_semaphore()
    peers = [xz_peer(o)[1] for o in range(1, 16)] + [core_peer] + [y_peer(o)[1] for o in range(1, 4)]
    for device in peers:
        pl.semaphore_signal(barrier, inc=1, device_id=device, device_id_type=MESH)
    keep(train, raw_rows, load_sem.at[0])
    keep(owner_map, owners, load_sem.at[1])
    pl.semaphore_wait(barrier, len(peers))

    def send_targets():
        for o in FAR_FIRST:
            other, device = dp_peer(o)
            send(target.at[:, columns(other)], all_targets.at[dp], target_sem, 0, device)
        keep(target.at[:, columns(dp)], all_targets.at[dp], target_sem.at[1, 0])

    def send_proj(i):
        rows = pl.ds(i * 16, 16)
        for o in FAR_FIRST:
            other, device = dp_peer(o)
            send(proj.at[rows, columns(other)], all_proj.at[i, dp], proj_sem, i, device)
        keep(proj.at[rows, columns(dp)], all_proj.at[i, dp], proj_sem.at[1, i])

    def send_moments():
        for o in FAR_FIRST:
            other, device = dp_peer(o)
            send(first.at[0], all_first.at[dp], mom_sem, 0, device)
            send(second.at[0], all_second.at[dp], mom_sem, 1, device)
        keep(first.at[0], all_first.at[dp], mom_sem.at[1, 0])
        keep(second.at[0], all_second.at[dp], mom_sem.at[1, 1])

    def piece_of(k, half):
        if k < LAST:
            return half * DEPTH, DEPTH, all_rows.at[k * 2 + half]
        return (COLS - SHORT, SHORT, last_short) if half else (0, COLS - SHORT, last_long)

    def send_rows(k, half):
        rows, at = pl.ds(k * 16, 16), k * 2 + half
        start, width, there = piece_of(k, half)

        def some(owner):
            return sorted_rows.at[rows, pl.ds(owner * COLS + start, width)]

        for o in FAR_FIRST:
            other, device = dp_peer(o)
            send(some(other), there.at[dp], row_sem, at, device)
        keep(some(dp), there.at[dp], row_sem.at[1, at])

    def sort_rows():
        wait(raw_rows, load_sem.at[0])
        pick = one_hot(64, lambda r: (r & 15) * 4 + (r >> 4))

        @pl.loop(0, 16)
        def _(t):
            cols = pl.ds(pl.multiple_of(t * 1024, 1024), 1024)
            sorted_rows[:, cols] = jnp.dot(
                pick, raw_rows[:, cols], preferred_element_type=F32
            ).astype(BF16)

    def regroup_targets():
        wait(all_targets, target_sem.at[1, 0])
        regroup = one_hot(
            256,
            lambda r: bits(r, 1, 3) * 32 + bits(r, 4, 1) * 16 + bits(r, 5, 2) * 4
            + bits(r, 7, 1) * 2 + bits(r, 0, 1),
        )

        @pl.loop(0, 8)
        def _(t):
            cols = pl.ds(pl.multiple_of(t * 256, 256), 256)
            target_lhs[:, cols] = jnp.dot(
                regroup, all_targets[:, :, cols].reshape(256, 256), preferred_element_type=F32
            ).astype(BF16)

    def transpose(i):
        wait(all_proj.at[i], proj_sem.at[1, i])
        same = one_hot(256, lambda r: r)
        for t in range(8):
            at = slice(t * 256, (t + 1) * 256)
            columns_of[at, i * 128 : (i + 1) * 128] = lax.dot_general(
                same, all_proj[i, :, :, at].reshape(128, 256), (((1,), (1,)), ((), ())),
                preferred_element_type=F32,
            ).astype(BF16)

    def multiply_targets(h):
        target_part[h] = jnp.dot(
            target_lhs[...], columns_of[:, h * HALF : (h + 1) * HALF], preferred_element_type=F32
        )
        away = pl.ds((1 - core) * 128, 128)
        send(target_part.at[h, away], target_from_core.at[h], core_sem, h, core_peer)

    def multiply(k, half):
        at = k * 2 + half
        start, width, here = piece_of(k, half)
        wait(here, row_sem.at[1, at])

        @pl.loop(0, 8)
        def _(s):
            for t in range(width // 512):
                cols = slice(t * 512, (t + 1) * 512)
                own = slice(start + t * 512, start + (t + 1) * 512)
                g = here[s, :, cols].astype(F32)
                upper = first_row[:, own] + 0.1 * g
                lower = jnp.sqrt(second_row[:, own] + 0.001 * g * g) + 1e-08
                mixed[s, :, cols] = (upper / lower).astype(BF16)

        for t in range(width // 512):
            cols = slice(t * 512, (t + 1) * 512)
            lhs[:, cols] = jnp.dot(
                regroup, mixed[:, :, cols].reshape(128, 512), preferred_element_type=F32
            ).astype(BF16)
        away = pl.ds((1 - core) * 64, 64)
        for h in range(2):
            cols = slice(h * HALF, (h + 1) * HALF)
            done = jnp.dot(
                lhs[:, 0:width], columns_of[start : start + width, cols],
                preferred_element_type=F32,
            )
            part[k, :, cols] = done if half == 0 else part[k, :, cols] + done
            if half == 1 and k == LAST:
                last_part[h] = part[k, away, cols].astype(BF16)
                send(last_part.at[h], last_from_core.at[h], last_core_sem, h, core_peer)
        if half == 1 and k < LAST:
            send(part.at[k, away], from_core.at[k], core_sem, 2 + k, core_peer)

    def add_core(g):
        if g < 2:
            here, there, total, arrived, k, rows = (
                target_part, target_from_core, target_by_y, target_from_y, g, 32,
            )
        else:
            here, there, total, arrived, k, rows = part, from_core, by_y, from_y, g - 2, 16
        wait(there.at[k], core_sem.at[1, g])

        @pl.loop(0, 4)
        def _(t):
            at = pl.ds(t * rows, rows)
            total[k, at] = here[k, pl.ds((core * 4 + t) * rows, rows)] + there[k, at]

        for o in (2, 1, 3):
            other, device = y_peer(o)
            send(total.at[k, pl.ds(other * rows, rows)], arrived.at[k, o - 1], y_sem, g, device)

    def add_core_last(h):
        cols = slice(h * HALF, (h + 1) * HALF)
        wait(last_from_core.at[h], last_core_sem.at[1, h])
        total = part[LAST, pl.ds(core * 64, 64), cols] + last_from_core[h].astype(F32)
        by_y[LAST, :, cols] = total
        last_by_y[h] = total.astype(BF16)
        for o in (2, 1, 3):
            other, device = y_peer(o)
            rows = pl.ds(other * 16, 16)
            send(last_by_y.at[h, rows], last_from_y.at[h, o - 1], last_y_sem, h, device)

    def add_y(g):
        if g == 5:
            total, k, rows = by_y, LAST, 16
            for h in range(2):
                wait(last_from_y.at[h], last_y_sem.at[1, h])
        elif g < 2:
            total, arrived, k, rows = target_by_y, target_from_y, g, 32
        else:
            total, arrived, k, rows = by_y, from_y, g - 2, 16
        done = total[k, pl.ds(y * rows, rows)]
        if g < 5:
            wait(arrived.at[k], y_sem.at[1, g])
            done = done + arrived[k, 0] + arrived[k, 1] + arrived[k, 2]
        else:
            for o in range(3):
                both = [last_from_y[h, o].astype(F32) for h in range(2)]
                done = done + jnp.concatenate(both, axis=1)
        tiles = 128 // rows
        for s in range(tiles):
            by_xz[g, pl.ds(s, rows, stride=tiles), :] = done[:, s * 128 : (s + 1) * 128]
        for o in XZ_FAR_FIRST:
            other, device = xz_peer(o)
            send(by_xz.at[g, pl.ds(other * 8, 8)], from_xz.at[g, pl.ds(o * 8 - 8, 8)], xz_sem, g, device)

    def add_xz(g):
        wait(from_xz.at[g], xz_sem.at[1, g])
        f = by_xz[g, pl.ds(place * 8, 8)]
        for o in range(15):
            f = f + from_xz[g, o * 8 : o * 8 + 8]
        return f

    spot = (core * 4 + y) * 16 + place

    def gather_xz(h):
        mine = raw_unit.at[h, pl.ds(spot * 8, 8)]
        raw_unit[h, pl.ds(spot * 8, 8)] = add_xz(h)
        for o in XZ_FAR_FIRST:
            send(mine, mine, gather_sem, h * 3, xz_peer(o)[1])

    def gather_y(h):
        wait(raw_unit.at[h, pl.ds(0, 120)], gather_sem.at[1, h * 3])
        mine = raw_unit.at[h, pl.ds((core * 4 + y) * 128, 128)]
        for o in (2, 1, 3):
            send(mine, mine, gather_sem, h * 3 + 1, y_peer(o)[1])

    def gather_core(h):
        wait(raw_unit.at[h, pl.ds(0, 384)], gather_sem.at[1, h * 3 + 1])
        mine = raw_unit.at[h, pl.ds(core * 512, 512)]
        send(mine, mine, gather_sem, h * 3 + 2, core_peer)

    def arrange():
        for h in range(2):
            wait(raw_unit.at[h, pl.ds(0, 512)], gather_sem.at[1, h * 3 + 2])
        natural = one_hot(
            256,
            lambda r: bits(r, 0, 1) * 128 + bits(r, 1, 1) * 64 + bits(r, 2, 2) * 16
            + bits(r, 4, 1) * 8 + bits(r, 5, 3),
            along=1,
        )

        def piece(h, s, c):
            return raw_unit[h, pl.ds(c * 4 + s, 128, stride=8), :]

        scale = []
        for c in range(2):
            squares = jnp.zeros((128, 128), F32)
            for h in range(2):
                for s in range(4):
                    f = piece(h, s, c)
                    squares = squares + f * f
            mean = jnp.sum(squares, axis=1, keepdims=True) / FEATS
            scale.append(lax.rsqrt(mean + 1e-06))
        for h in range(2):
            for s in range(4):
                f = jnp.concatenate([(piece(h, s, c) * scale[c]).T for c in range(2)], axis=1)
                high = f.astype(BF16)
                low = (f - high.astype(F32)).astype(BF16)
                at = slice(h * HALF + s * 128, h * HALF + (s + 1) * 128)
                unit_cat[at, 0:256] = jnp.dot(high, natural, preferred_element_type=F32).astype(BF16)
                unit_cat[at, 256:512] = jnp.dot(low, natural, preferred_element_type=F32).astype(BF16)

    def train_row(g):
        f = add_xz(g)
        mean = jnp.sum(f * f, keepdims=True) / FEATS
        own_rows[(g - 2) * 8 : (g - 1) * 8] = f * lax.rsqrt(mean + 1e-06)

    def sent():
        wait(all_targets.at[pl.ds(0, 7)], target_sem.at[0, 0])
        wait(all_first.at[pl.ds(0, 7)], mom_sem.at[0, 0])
        wait(all_second.at[pl.ds(0, 7)], mom_sem.at[0, 1])
        for i in range(PIECES):
            wait(all_proj.at[i, pl.ds(0, 7)], proj_sem.at[0, i])
        for h in range(2):
            wait(target_from_core.at[h], core_sem.at[0, h])
            wait(target_from_y.at[h], y_sem.at[0, h])
            wait(from_xz.at[h], xz_sem.at[0, h])
            wait(raw_unit.at[h, pl.ds(0, 120)], gather_sem.at[0, h * 3])
            wait(raw_unit.at[h, pl.ds(0, 384)], gather_sem.at[0, h * 3 + 1])
            wait(raw_unit.at[h, pl.ds(0, 512)], gather_sem.at[0, h * 3 + 2])
        for h in range(2):
            wait(piece_of(LAST, h)[2].at[pl.ds(0, 7)], row_sem.at[0, LAST * 2 + h])
            wait(last_from_core.at[h], last_core_sem.at[0, h])
            wait(last_from_y.at[h], last_y_sem.at[0, h])
        for k in range(LAST):
            for h in range(2):
                wait(all_rows.at[k * 2 + h, pl.ds(0, 7)], row_sem.at[0, k * 2 + h])
            wait(from_core.at[k], core_sem.at[0, 2 + k])
            wait(from_y.at[k], y_sem.at[0, 2 + k])
            wait(from_xz.at[2 + k], xz_sem.at[0, 2 + k])

    send_targets()
    send_proj(0)
    send_moments()
    send_proj(1)
    own_rows[...] = jnp.zeros_like(own_rows)
    sort_rows()
    regroup_targets()
    send_proj(2)
    transpose(0)
    send_proj(3)
    transpose(1)
    send_proj(4)
    wait(all_first, mom_sem.at[1, 0])
    wait(all_second, mom_sem.at[1, 1])
    pltpu.make_async_copy(owner_map, owners, load_sem.at[1]).wait()
    owner = owners[0, dp]
    first_row = 0.9 * all_first[owner]
    second_row = 0.999 * all_second[owner]
    regroup = one_hot(
        128, lambda r: bits(r, 0, 3) * 16 + bits(r, 3, 1) * 8 + bits(r, 4, 2) * 2 + bits(r, 6, 1)
    )

    transpose(2)
    send_proj(5)
    transpose(3)
    multiply_targets(0)
    send_proj(6)
    add_core(0)
    transpose(4)
    send_proj(7)
    transpose(5)
    add_y(0)
    send_rows(0, 0)
    send_rows(0, 1)
    transpose(6)
    send_rows(1, 0)
    transpose(7)
    multiply_targets(1)
    gather_xz(0)
    send_rows(1, 1)
    add_core(1)
    multiply(0, 0)
    multiply(0, 1)
    add_y(1)
    send_rows(2, 0)
    gather_y(0)
    send_rows(2, 1)
    add_core(2)
    multiply(1, 0)
    multiply(1, 1)
    gather_xz(1)
    send_rows(3, 0)
    send_rows(3, 1)
    add_core(3)
    gather_core(0)
    multiply(2, 0)
    multiply(2, 1)
    gather_y(1)
    add_core(4)
    multiply(3, 0)
    multiply(3, 1)
    add_core_last(0)
    add_core_last(1)
    add_y(2)
    add_y(3)
    gather_core(1)
    add_y(4)
    arrange()
    add_y(5)
    train_row(2)
    train_row(3)
    sent()
    train_row(4)
    train_row(5)

    rows = jnp.concatenate([own_rows[pl.ds(s, 8, stride=8), :] for s in range(8)], axis=1)
    high = rows.astype(BF16)
    low = (rows - high.astype(F32)).astype(BF16)
    product = jnp.dot(
        jnp.concatenate([high, low], axis=0), unit_cat[...], preferred_element_type=F32
    )
    scaled = product[0:8, 0:256] + (product[8:16, 0:256] + product[0:8, 256:512])
    out[...] = scaled[0:4] / math.sqrt(FEATS)

    wait(from_xz.at[5], xz_sem.at[0, 5])


def per_device(train, target, proj, first, second, owners):
    vmem = pltpu.VMEM
    dma = pltpu.SemaphoreType.DMA
    anywhere = pl.BlockSpec(memory_space=pl.ANY)
    return pl.pallas_call(
        kernel,
        out_shape=jax.ShapeDtypeStruct((4, 256), F32),
        in_specs=[anywhere] * 6,
        out_specs=pl.BlockSpec(memory_space=pltpu.VMEM),
        scratch_shapes=[
            pltpu.SMEM((1, 8), jnp.int32),
            vmem((64, 16384), BF16),
            vmem((64, 16384), BF16),
            vmem((8, 32, COLS), BF16),
            vmem((PIECES, 8, 16, COLS), BF16),
            vmem((COLS, FEATS), BF16),
            vmem((LAST * 2, 8, 16, DEPTH), BF16),
            vmem((8, 16, COLS - SHORT), BF16),
            vmem((8, 16, SHORT), BF16),
            vmem((8, 1, COLS), F32),
            vmem((8, 1, COLS), F32),
            vmem((256, COLS), BF16),
            vmem((8, 16, COLS - SHORT), BF16),
            vmem((128, COLS - SHORT), BF16),
            vmem((2, 256, HALF), F32),
            vmem((2, 128, HALF), F32),
            vmem((2, 128, HALF), F32),
            vmem((2, 3, 32, HALF), F32),
            vmem((GROUPS, 128, FEATS), F32),
            vmem((LAST, 64, FEATS), F32),
            vmem((GROUPS, 64, FEATS), F32),
            vmem((LAST, 3, 16, FEATS), F32),
            vmem((2, 64, HALF), BF16),
            vmem((2, 64, HALF), BF16),
            vmem((2, 64, HALF), BF16),
            vmem((2, 3, 16, HALF), BF16),
            vmem((2 + GROUPS, 128, 128), F32),
            vmem((2 + GROUPS, 120, 128), F32),
            vmem((2, 1024, 128), F32),
            vmem((FEATS, 512), BF16),
            vmem((64, 128), F32),
            dma((2,)),
            dma((2, 2)),
            dma((2, 1)),
            dma((2, PIECES)),
            dma((2, GROUPS * 2)),
            dma((2, 2 + LAST)),
            dma((2, 2 + LAST)),
            dma((2, 2 + GROUPS)),
            dma((2, 6)),
            dma((2, 2)),
            dma((2, 2)),
        ],
        compiler_params=pltpu.CompilerParams(
            collective_id=0, has_side_effects=True, vmem_limit_bytes=40 * 2**20
        ),
    )(*(pltpu.with_memory_space_constraint(a, pltpu.HBM) for a in (train, target, proj, first, second, owners)))


def solution(mesh):
    placed = (
        P("dp", "param"),
        P("dp", "param"),
        P("dp", "param"),
        P("param", "dp", None),
        P("param", "dp", None),
        P("param", None),
    )
    return jax.shard_map(
        per_device, mesh=mesh, in_specs=placed, out_specs=P(("dp", "param"), None), check_vma=False
    )
```

```python
import math

import jax
import jax.numpy as jnp
from jax import lax
from jax.experimental import pallas as pl
from jax.experimental.pallas import tpu as pltpu
from jax.sharding import PartitionSpec as P

MESH = pl.DeviceIdType.MESH
F32, BF16 = jnp.float32, jnp.bfloat16
COLS = 2048
FEATS = 1024
HALF = 512
DEPTH = COLS // 2
SHORT = 512
PIECES = 8
GROUPS = 4
LAST = GROUPS - 1
FAR_FIRST = (2, 6, 5, 7, 1, 3, 4)
XZ_FAR_FIRST = (10, 14, 13, 15, 9, 11, 12, 2, 6, 8, 5, 7, 1, 3, 4)


def one_hot(rows, source_of, along=0):
    r = lax.broadcasted_iota(jnp.int32, (rows, rows), along)
    s = lax.broadcasted_iota(jnp.int32, (rows, rows), 1 - along)
    return jnp.where(source_of(r) == s, 1.0, 0.0).astype(BF16)


def bits(r, low, width):
    return (r >> low) & ((1 << width) - 1)


def kernel(
    train, target, proj, first, second, owner_map,
    out,
    owners, raw_rows, sorted_rows, all_targets, all_proj, columns_of, all_rows, last_long, last_short, all_first, all_second,
    target_lhs, mixed, lhs,
    target_part, target_from_core, target_by_y, target_from_y,
    part, from_core, by_y, from_y, last_part, last_from_core, last_by_y, last_from_y, by_xz, from_xz, raw_unit, unit_cat, own_rows,
    load_sem, mom_sem, target_sem, proj_sem, row_sem, core_sem, y_sem, xz_sem, gather_sem,
    last_core_sem, last_y_sem,
):
    dp = lax.axis_index("dp")
    param = lax.axis_index("param")
    x_hi, y, core = param // 8, (param // 2) % 4, param % 2
    place = x_hi * 8 + dp

    def dp_peer(o):
        return (dp + o) % 8, {"dp": (dp + o) % 8, "param": param}

    core_peer = {"dp": dp, "param": x_hi * 8 + y * 2 + (1 - core)}

    def y_peer(o):
        other = (y + o) % 4
        return other, {"dp": dp, "param": x_hi * 8 + other * 2 + core}

    def xz_peer(o):
        far, near = (x_hi + o // 8) % 2, (dp + o % 8) % 8
        return far * 8 + near, {"dp": near, "param": far * 8 + y * 2 + core}

    def send(src, dst, sems, at, device):
        pltpu.make_async_remote_copy(
            src_ref=src, dst_ref=dst, send_sem=sems.at[0, at], recv_sem=sems.at[1, at],
            device_id=device, device_id_type=MESH,
        ).start()

    def keep(src, dst, sem):
        pltpu.make_async_copy(src, dst, sem).start()

    def wait(ref, sem):
        pltpu.make_async_copy(ref, ref, sem).wait()

    def columns(owner):
        return pl.ds(owner * COLS, COLS)

    barrier = pltpu.get_barrier_semaphore()
    peers = [xz_peer(o)[1] for o in XZ_FAR_FIRST] + [y_peer(o)[1] for o in (2, 1, 3)] + [core_peer]
    for device in peers:
        pl.semaphore_signal(barrier, inc=1, device_id=device, device_id_type=MESH)
    keep(train, raw_rows, load_sem.at[0])
    keep(owner_map, owners, load_sem.at[1])
    pl.semaphore_wait(barrier, len(peers))

    def send_targets():
        for o in FAR_FIRST:
            other, device = dp_peer(o)
            send(target.at[:, columns(other)], all_targets.at[dp], target_sem, 0, device)
        keep(target.at[:, columns(dp)], all_targets.at[dp], target_sem.at[1, 0])

    def send_proj(i):
        rows = pl.ds(i * 16, 16)
        for o in FAR_FIRST:
            other, device = dp_peer(o)
            send(proj.at[rows, columns(other)], all_proj.at[i, dp], proj_sem, i, device)
        keep(proj.at[rows, columns(dp)], all_proj.at[i, dp], proj_sem.at[1, i])

    def send_moments():
        for o in FAR_FIRST:
            other, device = dp_peer(o)
            send(first.at[0], all_first.at[dp], mom_sem, 0, device)
            send(second.at[0], all_second.at[dp], mom_sem, 1, device)
        keep(first.at[0], all_first.at[dp], mom_sem.at[1, 0])
        keep(second.at[0], all_second.at[dp], mom_sem.at[1, 1])

    def piece_of(k, half):
        if k < LAST:
            return half * DEPTH, DEPTH, all_rows.at[k * 2 + half]
        return (COLS - SHORT, SHORT, last_short) if half else (0, COLS - SHORT, last_long)

    def send_rows(k, half):
        rows, at = pl.ds(k * 16, 16), k * 2 + half
        start, width, there = piece_of(k, half)

        def some(owner):
            return sorted_rows.at[rows, pl.ds(owner * COLS + start, width)]

        for o in FAR_FIRST:
            other, device = dp_peer(o)
            send(some(other), there.at[dp], row_sem, at, device)
        keep(some(dp), there.at[dp], row_sem.at[1, at])

    def sort_rows():
        wait(raw_rows, load_sem.at[0])
        pick = one_hot(64, lambda r: (r & 15) * 4 + (r >> 4))

        @pl.loop(0, 16)
        def _(t):
            cols = pl.ds(pl.multiple_of(t * 1024, 1024), 1024)
            sorted_rows[:, cols] = jnp.dot(
                pick, raw_rows[:, cols], preferred_element_type=F32
            ).astype(BF16)

    def regroup_targets():
        wait(all_targets, target_sem.at[1, 0])
        regroup = one_hot(
            256,
            lambda r: bits(r, 1, 3) * 32 + bits(r, 4, 1) * 16 + bits(r, 5, 2) * 4
            + bits(r, 7, 1) * 2 + bits(r, 0, 1),
        )

        @pl.loop(0, 8)
        def _(t):
            cols = pl.ds(pl.multiple_of(t * 256, 256), 256)
            target_lhs[:, cols] = jnp.dot(
                regroup, all_targets[:, :, cols].reshape(256, 256), preferred_element_type=F32
            ).astype(BF16)

    def transpose(i):
        wait(all_proj.at[i], proj_sem.at[1, i])
        same = one_hot(256, lambda r: r)
        for t in range(8):
            at = slice(t * 256, (t + 1) * 256)
            columns_of[at, i * 128 : (i + 1) * 128] = lax.dot_general(
                same, all_proj[i, :, :, at].reshape(128, 256), (((1,), (1,)), ((), ())),
                preferred_element_type=F32,
            ).astype(BF16)

    def multiply_targets(h):
        target_part[h] = jnp.dot(
            target_lhs[...], columns_of[:, h * HALF : (h + 1) * HALF], preferred_element_type=F32
        )
        away = pl.ds((1 - core) * 128, 128)
        send(target_part.at[h, away], target_from_core.at[h], core_sem, h, core_peer)

    def multiply(k, half):
        at = k * 2 + half
        start, width, here = piece_of(k, half)
        wait(here, row_sem.at[1, at])

        @pl.loop(0, 8)
        def _(s):
            for t in range(width // 512):
                cols = slice(t * 512, (t + 1) * 512)
                own = slice(start + t * 512, start + (t + 1) * 512)
                g = here[s, :, cols].astype(F32)
                upper = first_row[:, own] + 0.1 * g
                lower = jnp.sqrt(second_row[:, own] + 0.001 * g * g) + 1e-08
                mixed[s, :, cols] = (upper / lower).astype(BF16)

        for t in range(width // 512):
            cols = slice(t * 512, (t + 1) * 512)
            lhs[:, cols] = jnp.dot(
                regroup, mixed[:, :, cols].reshape(128, 512), preferred_element_type=F32
            ).astype(BF16)
        away = pl.ds((1 - core) * 64, 64)
        for h in range(2):
            cols = slice(h * HALF, (h + 1) * HALF)
            done = jnp.dot(
                lhs[:, 0:width], columns_of[start : start + width, cols],
                preferred_element_type=F32,
            )
            part[k, :, cols] = done if half == 0 else part[k, :, cols] + done
            if half == 1 and k == LAST:
                last_part[h] = part[k, away, cols].astype(BF16)
                send(last_part.at[h], last_from_core.at[h], last_core_sem, h, core_peer)
        if half == 1 and k < LAST:
            send(part.at[k, away], from_core.at[k], core_sem, 2 + k, core_peer)

    def add_core(g):
        if g < 2:
            here, there, total, arrived, k, rows = (
                target_part, target_from_core, target_by_y, target_from_y, g, 32,
            )
        else:
            here, there, total, arrived, k, rows = part, from_core, by_y, from_y, g - 2, 16
        wait(there.at[k], core_sem.at[1, g])

        @pl.loop(0, 4)
        def _(t):
            at = pl.ds(t * rows, rows)
            total[k, at] = here[k, pl.ds((core * 4 + t) * rows, rows)] + there[k, at]

        for o in (2, 1, 3):
            other, device = y_peer(o)
            send(total.at[k, pl.ds(other * rows, rows)], arrived.at[k, o - 1], y_sem, g, device)

    def add_core_last(h):
        cols = slice(h * HALF, (h + 1) * HALF)
        wait(last_from_core.at[h], last_core_sem.at[1, h])
        total = part[LAST, pl.ds(core * 64, 64), cols] + last_from_core[h].astype(F32)
        by_y[LAST, :, cols] = total
        last_by_y[h] = total.astype(BF16)
        for o in (2, 1, 3):
            other, device = y_peer(o)
            rows = pl.ds(other * 16, 16)
            send(last_by_y.at[h, rows], last_from_y.at[h, o - 1], last_y_sem, h, device)

    def add_y(g):
        if g == 5:
            total, k, rows = by_y, LAST, 16
            for h in range(2):
                wait(last_from_y.at[h], last_y_sem.at[1, h])
        elif g < 2:
            total, arrived, k, rows = target_by_y, target_from_y, g, 32
        else:
            total, arrived, k, rows = by_y, from_y, g - 2, 16
        done = total[k, pl.ds(y * rows, rows)]
        if g < 5:
            wait(arrived.at[k], y_sem.at[1, g])
            done = done + arrived[k, 0] + arrived[k, 1] + arrived[k, 2]
        else:
            for o in range(3):
                both = [last_from_y[h, o].astype(F32) for h in range(2)]
                done = done + jnp.concatenate(both, axis=1)
        tiles = 128 // rows
        for s in range(tiles):
            by_xz[g, pl.ds(s, rows, stride=tiles), :] = done[:, s * 128 : (s + 1) * 128]
        for o in XZ_FAR_FIRST:
            other, device = xz_peer(o)
            send(by_xz.at[g, pl.ds(other * 8, 8)], from_xz.at[g, pl.ds(o * 8 - 8, 8)], xz_sem, g, device)

    def add_xz(g):
        wait(from_xz.at[g], xz_sem.at[1, g])
        f = by_xz[g, pl.ds(place * 8, 8)]
        for o in range(15):
            f = f + from_xz[g, o * 8 : o * 8 + 8]
        return f

    spot = (core * 4 + y) * 16 + place

    def gather_xz(h):
        mine = raw_unit.at[h, pl.ds(spot * 8, 8)]
        raw_unit[h, pl.ds(spot * 8, 8)] = add_xz(h)
        for o in XZ_FAR_FIRST:
            send(mine, mine, gather_sem, h * 3, xz_peer(o)[1])

    def gather_y(h):
        wait(raw_unit.at[h, pl.ds(0, 120)], gather_sem.at[1, h * 3])
        mine = raw_unit.at[h, pl.ds((core * 4 + y) * 128, 128)]
        for o in (2, 1, 3):
            send(mine, mine, gather_sem, h * 3 + 1, y_peer(o)[1])

    def gather_core(h):
        wait(raw_unit.at[h, pl.ds(0, 384)], gather_sem.at[1, h * 3 + 1])
        mine = raw_unit.at[h, pl.ds(core * 512, 512)]
        send(mine, mine, gather_sem, h * 3 + 2, core_peer)

    def arrange():
        for h in range(2):
            wait(raw_unit.at[h, pl.ds(0, 512)], gather_sem.at[1, h * 3 + 2])
        natural = one_hot(
            256,
            lambda r: bits(r, 0, 1) * 128 + bits(r, 1, 1) * 64 + bits(r, 2, 2) * 16
            + bits(r, 4, 1) * 8 + bits(r, 5, 3),
            along=1,
        )

        def piece(h, s, c):
            return raw_unit[h, pl.ds(c * 4 + s, 128, stride=8), :]

        scale = []
        for c in range(2):
            squares = jnp.zeros((128, 128), F32)
            for h in range(2):
                for s in range(4):
                    f = piece(h, s, c)
                    squares = squares + f * f
            mean = jnp.sum(squares, axis=1, keepdims=True) / FEATS
            scale.append(lax.rsqrt(mean + 1e-06))
        for h in range(2):
            for s in range(4):
                f = jnp.concatenate([(piece(h, s, c) * scale[c]).T for c in range(2)], axis=1)
                high = f.astype(BF16)
                low = (f - high.astype(F32)).astype(BF16)
                at = slice(h * HALF + s * 128, h * HALF + (s + 1) * 128)
                unit_cat[at, 0:256] = jnp.dot(high, natural, preferred_element_type=F32).astype(BF16)
                unit_cat[at, 256:512] = jnp.dot(low, natural, preferred_element_type=F32).astype(BF16)

    def train_row(g):
        f = add_xz(g)
        mean = jnp.sum(f * f, keepdims=True) / FEATS
        own_rows[(g - 2) * 8 : (g - 1) * 8] = f * lax.rsqrt(mean + 1e-06)

    def sent():
        wait(all_targets.at[pl.ds(0, 7)], target_sem.at[0, 0])
        wait(all_first.at[pl.ds(0, 7)], mom_sem.at[0, 0])
        wait(all_second.at[pl.ds(0, 7)], mom_sem.at[0, 1])
        for i in range(PIECES):
            wait(all_proj.at[i, pl.ds(0, 7)], proj_sem.at[0, i])
        for h in range(2):
            wait(target_from_core.at[h], core_sem.at[0, h])
            wait(target_from_y.at[h], y_sem.at[0, h])
            wait(from_xz.at[h], xz_sem.at[0, h])
            wait(raw_unit.at[h, pl.ds(0, 120)], gather_sem.at[0, h * 3])
            wait(raw_unit.at[h, pl.ds(0, 384)], gather_sem.at[0, h * 3 + 1])
            wait(raw_unit.at[h, pl.ds(0, 512)], gather_sem.at[0, h * 3 + 2])
        for h in range(2):
            wait(piece_of(LAST, h)[2].at[pl.ds(0, 7)], row_sem.at[0, LAST * 2 + h])
            wait(last_from_core.at[h], last_core_sem.at[0, h])
            wait(last_from_y.at[h], last_y_sem.at[0, h])
        for k in range(LAST):
            for h in range(2):
                wait(all_rows.at[k * 2 + h, pl.ds(0, 7)], row_sem.at[0, k * 2 + h])
            wait(from_core.at[k], core_sem.at[0, 2 + k])
            wait(from_y.at[k], y_sem.at[0, 2 + k])
            wait(from_xz.at[2 + k], xz_sem.at[0, 2 + k])

    send_targets()
    send_proj(0)
    send_moments()
    send_proj(1)
    own_rows[...] = jnp.zeros_like(own_rows)
    sort_rows()
    regroup_targets()
    send_proj(2)
    transpose(0)
    send_proj(3)
    transpose(1)
    send_proj(4)
    wait(all_first, mom_sem.at[1, 0])
    wait(all_second, mom_sem.at[1, 1])
    pltpu.make_async_copy(owner_map, owners, load_sem.at[1]).wait()
    owner = owners[0, dp]
    first_row = 0.9 * all_first[owner]
    second_row = 0.999 * all_second[owner]
    regroup = one_hot(
        128, lambda r: bits(r, 0, 3) * 16 + bits(r, 3, 1) * 8 + bits(r, 4, 2) * 2 + bits(r, 6, 1)
    )

    transpose(2)
    send_proj(5)
    transpose(3)
    multiply_targets(0)
    send_proj(6)
    add_core(0)
    transpose(4)
    send_proj(7)
    transpose(5)
    add_y(0)
    send_rows(0, 0)
    send_rows(0, 1)
    transpose(6)
    send_rows(1, 0)
    transpose(7)
    multiply_targets(1)
    gather_xz(0)
    send_rows(1, 1)
    add_core(1)
    multiply(0, 0)
    multiply(0, 1)
    add_y(1)
    send_rows(2, 0)
    gather_y(0)
    send_rows(2, 1)
    add_core(2)
    multiply(1, 0)
    multiply(1, 1)
    gather_xz(1)
    send_rows(3, 0)
    send_rows(3, 1)
    add_core(3)
    gather_core(0)
    multiply(2, 0)
    multiply(2, 1)
    gather_y(1)
    add_core(4)
    multiply(3, 0)
    multiply(3, 1)
    add_core_last(0)
    add_core_last(1)
    add_y(2)
    add_y(3)
    gather_core(1)
    add_y(4)
    arrange()
    add_y(5)
    train_row(2)
    train_row(3)
    sent()
    train_row(4)
    train_row(5)

    rows = jnp.concatenate([own_rows[pl.ds(s, 8, stride=8), :] for s in range(8)], axis=1)
    high = rows.astype(BF16)
    low = (rows - high.astype(F32)).astype(BF16)
    product = jnp.dot(
        jnp.concatenate([high, low], axis=0), unit_cat[...], preferred_element_type=F32
    )
    scaled = product[0:8, 0:256] + (product[8:16, 0:256] + product[0:8, 256:512])
    out[...] = scaled[0:4] / math.sqrt(FEATS)

    wait(from_xz.at[5], xz_sem.at[0, 5])


def per_device(train, target, proj, first, second, owners):
    vmem = pltpu.VMEM
    dma = pltpu.SemaphoreType.DMA
    anywhere = pl.BlockSpec(memory_space=pl.ANY)
    return pl.pallas_call(
        kernel,
        out_shape=jax.ShapeDtypeStruct((4, 256), F32),
        in_specs=[anywhere] * 6,
        out_specs=pl.BlockSpec(memory_space=pltpu.VMEM),
        scratch_shapes=[
            pltpu.SMEM((1, 8), jnp.int32),
            vmem((64, 16384), BF16),
            vmem((64, 16384), BF16),
            vmem((8, 32, COLS), BF16),
            vmem((PIECES, 8, 16, COLS), BF16),
            vmem((COLS, FEATS), BF16),
            vmem((LAST * 2, 8, 16, DEPTH), BF16),
            vmem((8, 16, COLS - SHORT), BF16),
            vmem((8, 16, SHORT), BF16),
            vmem((8, 1, COLS), F32),
            vmem((8, 1, COLS), F32),
            vmem((256, COLS), BF16),
            vmem((8, 16, COLS - SHORT), BF16),
            vmem((128, COLS - SHORT), BF16),
            vmem((2, 256, HALF), F32),
            vmem((2, 128, HALF), F32),
            vmem((2, 128, HALF), F32),
            vmem((2, 3, 32, HALF), F32),
            vmem((GROUPS, 128, FEATS), F32),
            vmem((LAST, 64, FEATS), F32),
            vmem((GROUPS, 64, FEATS), F32),
            vmem((LAST, 3, 16, FEATS), F32),
            vmem((2, 64, HALF), BF16),
            vmem((2, 64, HALF), BF16),
            vmem((2, 64, HALF), BF16),
            vmem((2, 3, 16, HALF), BF16),
            vmem((2 + GROUPS, 128, 128), F32),
            vmem((2 + GROUPS, 120, 128), F32),
            vmem((2, 1024, 128), F32),
            vmem((FEATS, 512), BF16),
            vmem((64, 128), F32),
            dma((2,)),
            dma((2, 2)),
            dma((2, 1)),
            dma((2, PIECES)),
            dma((2, GROUPS * 2)),
            dma((2, 2 + LAST)),
            dma((2, 2 + LAST)),
            dma((2, 2 + GROUPS)),
            dma((2, 6)),
            dma((2, 2)),
            dma((2, 2)),
        ],
        compiler_params=pltpu.CompilerParams(
            collective_id=0, has_side_effects=True, vmem_limit_bytes=40 * 2**20
        ),
    )(*(pltpu.with_memory_space_constraint(a, pltpu.HBM) for a in (train, target, proj, first, second, owners)))


def solution(mesh):
    placed = (
        P("dp", "param"),
        P("dp", "param"),
        P("dp", "param"),
        P("param", "dp", None),
        P("param", "dp", None),
        P("param", None),
    )
    return jax.shard_map(
        per_device, mesh=mesh, in_specs=placed, out_specs=P(("dp", "param"), None), check_vma=False
    )
```
